32 devices in a mesh: tm: 16 (over z, y, core), rows: 2 (over x).
Axes of the slice: x: 2, y: 2, z: 4, core: 2. Of those that a mesh axis runs over, the one named last changes fastest.
Arguments:
- noisy_states: float32 [64, 2, 16, 256], P('tm', None, 'rows'), may hold values from -6 to 6
- noise_first: float32 [64, 2, 16, 256], P('tm', None, 'rows'), may hold values from -6 to 6
- noise_second: float32 [64, 2, 16, 256], P('tm', None, 'rows'), may hold values from -6 to 6
- conv_in: bfloat16 [9, 96, 18], replicated, may hold values from -0.5 to 0.5
- conv_out: bfloat16 [9, 2, 96], replicated, may hold values from -0.21875 to 0.21875
- level_embed: float32 [96], replicated, may hold values from -4 to 4
- obs_count: int32 [16, 2], P('tm', 'rows'), may hold values from 1 to 256, as said below
- obs_step: int32 [16, 2, 256], P('tm', 'rows'), may hold values from 0 to 3
- obs_row: int32 [16, 2, 256], P('tm', 'rows'), may hold values from 0 to 7
- obs_col: int32 [16, 2, 256], P('tm', 'rows'), may hold values from 0 to 255
- obs_value: float32 [16, 2, 256], P('tm', 'rows'), may hold values from -4 to 4
Outputs:
- final_states: float32 [64, 2, 16, 256], P('tm', None, 'rows')
The draws below stay inside these ranges and needn't reach their ends.
Inputs may be any that keep to these rules, and one draw needn't show every extreme that they name: `obs_count`: some block has exactly 256 live observations in every draw; the counts are skewed over blocks.
All inputs are finite; a program needn't handle non-finite values.
Results may differ from the reference program's by a relative error of at most 0.0014.
Values may be sent and summed in bfloat16 or wider, within the bound.
No kernel may reach another device: no remote copies, remote signals or barrier semaphores. Data moves between devices by JAX's collectives and lax.ppermute only.
A program may use at most 64 MiB of HBM per device.

```python
import jax
import jax.numpy as jnp
from jax import lax

T_DEV = 4
ROWS_DEV = 8
OBS_CAP = 256
COLS = 256
LAYERS = 2
K = 4
HID = 96
C_IN = 18
STEPS = 64
NY = 16
N_TM = 16
N_ROWS = 2


def draw_obs_count(key, part):
    first_key, second_key, third_key = jax.random.split(jax.random.fold_in(key, 17), 3)
    base_count = jax.random.randint(first_key, (N_TM * N_ROWS,), 1, OBS_CAP // 8 + 1)
    dense_pick = jax.random.randint(second_key, (N_TM * N_ROWS,), 0, 4)
    counts = jnp.minimum(base_count * jnp.where(dense_pick == 3, 8, 1), OBS_CAP)
    full_block = jax.random.randint(third_key, (), 0, N_TM * N_ROWS)
    counts = counts.at[full_block].set(OBS_CAP)
    return counts.reshape(N_TM, N_ROWS).astype(jnp.int32)


def plant(result, rng, smallest, largest):
    longest = result.shape.index(max(result.shape))
    spots = []
    for shift in (0, 1):
        where = [jax.random.randint(jax.random.fold_in(rng, axis), (), 0, length) for axis, length in enumerate(result.shape)]
        where[longest] = (where[longest] + shift) % result.shape[longest]
        spots.append(tuple(where))
    return result.at[spots[0]].set(smallest).at[spots[1]].set(largest)


def levels(stream_key, extent, cuts, low, largest):
    level, own = 1.0, jax.random.fold_in(stream_key, 6)
    for axis_at, shards_of in cuts:
        draws = jnp.exp(jax.random.uniform(jax.random.fold_in(own, axis_at), (shards_of,), jnp.float32, low / len(cuts), largest / len(cuts)))
        level = level * jnp.repeat(draws, extent[axis_at] // shards_of).reshape([-1 if axis == axis_at else 1 for axis in range(len(extent))])
    return level


def gaussian(key, shape, scale, limit, cuts=(), kind=jnp.bfloat16):
    loudness = levels(key, shape, cuts, -0.22, 0.18) if cuts else 1.0
    array = jax.random.normal(key, shape, jnp.float32) * scale * loudness
    return jnp.minimum(jnp.maximum(array, -limit), limit).astype(kind)


def setup_inputs(seed: int = 0) -> dict:
    arg_keys = jax.random.split(jax.random.key(seed), 12)
    return {
        "noisy_states": gaussian(arg_keys[0], (STEPS, LAYERS, NY, COLS), 1.0, 6.0, ((0, 16), (2, 2)), jnp.float32),
        "noise_first": gaussian(arg_keys[1], (STEPS, LAYERS, NY, COLS), 1.0, 6.0, ((0, 16), (2, 2)), jnp.float32),
        "noise_second": gaussian(arg_keys[2], (STEPS, LAYERS, NY, COLS), 1.0, 6.0, ((0, 16), (2, 2)), jnp.float32),
        "conv_in": gaussian(arg_keys[3], (9, HID, C_IN), (9 * C_IN) ** -0.5, 0.5),
        "conv_out": gaussian(arg_keys[4], (9, LAYERS, HID), (9 * HID) ** -0.5, 0.21875),
        "level_embed": gaussian(arg_keys[5], (HID,), 1.0, 4.0, (), jnp.float32),
        "obs_count": draw_obs_count(jax.random.fold_in(arg_keys[11], 71), 0),
        "obs_step": plant(jax.random.randint(arg_keys[7], (N_TM, N_ROWS, OBS_CAP), 0, T_DEV), jax.random.fold_in(arg_keys[7], 1), 0, T_DEV - 1).astype(jnp.int32),
        "obs_row": plant(jax.random.randint(arg_keys[8], (N_TM, N_ROWS, OBS_CAP), 0, ROWS_DEV), jax.random.fold_in(arg_keys[8], 1), 0, ROWS_DEV - 1).astype(jnp.int32),
        "obs_col": plant(jax.random.randint(arg_keys[9], (N_TM, N_ROWS, OBS_CAP), 0, COLS), jax.random.fold_in(arg_keys[9], 1), 0, COLS - 1).astype(jnp.int32),
        "obs_value": gaussian(arg_keys[10], (N_TM, N_ROWS, OBS_CAP), 1.0, 4.0, ((0, 16), (1, 2)), jnp.float32),
    }


LEVELS = (1.0, 0.5, 0.2)
OBS_NOISE = 0.1
COVARIANCE_GAIN = 0.5

def conv_periodic(window, weights):
    summed = jnp.zeros((weights.shape[1], window.shape[1], window.shape[2]), jnp.float32)
    for row_off in range(3):
        for col_off in range(3):
            shifted = jnp.roll(window, (1 - row_off, 1 - col_off), axis=(1, 2))
            summed = summed + jnp.einsum('oc,crw->orw', weights[3 * row_off + col_off].astype(jnp.float32), shifted.astype(jnp.float32))
    return summed

def reverse_step(current, noise_draw, level_now, level_next, conv_in, conv_out, level_embed, obs_count, obs_step, obs_row, obs_col, obs_value):
    scaled = (current / jnp.sqrt(1.0 + level_now ** 2)).astype(jnp.bfloat16)
    padded = jnp.pad(scaled, ((K, K), (0, 0), (0, 0), (0, 0)))

    def per_state(position):
        window = lax.dynamic_slice_in_dim(padded, position, 2 * K + 1, 0).reshape(C_IN, NY, COLS)
        hidden = jax.nn.silu(conv_periodic(window, conv_in) + level_now * level_embed[:, None, None]).astype(jnp.bfloat16)
        return conv_periodic(hidden, conv_out)
    net = lax.map(per_state, jnp.arange(STEPS, dtype=jnp.int32))
    denoised = current / (1.0 + level_now ** 2) + level_now / jnp.sqrt(1.0 + level_now ** 2) * net
    global_step = obs_step + (jnp.arange(N_TM, dtype=jnp.int32) * T_DEV)[:, None, None]
    global_row = obs_row + (jnp.arange(N_ROWS, dtype=jnp.int32) * ROWS_DEV)[None, :, None]
    active_slot = jnp.arange(OBS_CAP, dtype=jnp.int32)[None, None, :] < obs_count[:, :, None]
    picked = denoised[global_step, 0, global_row, obs_col]
    misfit = jnp.where(active_slot, (obs_value - picked) / (OBS_NOISE + COVARIANCE_GAIN * level_now ** 2), jnp.float32(0.0))
    guide = jnp.zeros(current.shape, jnp.float32).at[global_step, 0, global_row, obs_col].add(misfit)
    score = (denoised - current) / level_now ** 2 + guide
    spread = level_now ** 2 - level_next ** 2
    return current + spread * score + spread ** 0.5 * noise_draw

def reference(noisy_states, noise_first, noise_second, conv_in, conv_out, level_embed, obs_count, obs_step, obs_row, obs_col, obs_value):
    current = noisy_states
    for index_level, noise_draw in enumerate((noise_first, noise_second)):
        current = reverse_step(current, noise_draw, LEVELS[index_level], LEVELS[index_level + 1], conv_in, conv_out, level_embed, obs_count, obs_step, obs_row, obs_col, obs_value)
    return current
```

```python
import functools

import jax
import jax.numpy as jnp
from jax import lax
from jax.experimental import pallas as pl
from jax.experimental.pallas import tpu as pltpu
from jax.sharding import PartitionSpec as P

LEVELS = (1.0, 0.5, 0.2)
OBS_NOISE = 0.1
COVARIANCE_GAIN = 0.5

FL = 8
ROWS = 8
COLS = 256
HID = 96
FRAMES = 4
GROUP = 3 * FL
BLOCK = 80
DEPTH = 256
MSG_NOISE = ROWS * FL
MSG_OBS = MSG_NOISE + 4 * FL
MSG_ROWS = MSG_OBS + 16
NO_CELL = 64.0
VMEM = pl.BlockSpec(memory_space=pltpu.VMEM)
SMEM = pl.BlockSpec(memory_space=pltpu.SMEM)
F32 = jnp.float32
BF16 = jnp.bfloat16


def params():
    return pltpu.CompilerParams(vmem_limit_bytes=16 * 1024 * 1024)


def iota(shape, dim):
    return lax.broadcasted_iota(jnp.int32, shape, dim)


def split_halves(ref, halves_ref):
    halves_ref[0 : ROWS * FL, :] = ref[:, 0:128]
    halves_ref[ROWS * FL :, :] = ref[:, 128:256]


def row_of(halves_ref, row):
    left = halves_ref[pl.ds(row, FL, stride=ROWS), :]
    right = halves_ref[pl.ds(ROWS * FL + row, FL, stride=ROWS), :]
    return jnp.concatenate([left, right], axis=1)


def pack_kernel(
    count_ref, x_in, noise_in, step_ref, row_ref, col_ref, val_ref, msg_ref, x_ref, noise_ref
):
    split_halves(x_in, x_ref)
    split_halves(noise_in, noise_ref)
    inv = 1.0 / (1.0 + LEVELS[0] ** 2) ** 0.5
    for row in range(0, ROWS, 2):
        pair = jnp.concatenate([row_of(x_ref, row), row_of(x_ref, row + 1)], axis=0)
        msg_ref[row * FL : (row + 2) * FL, :] = (pair * inv).astype(BF16)
    for at, row in enumerate((0, ROWS - 2)):
        pair = jnp.concatenate([row_of(noise_ref, row), row_of(noise_ref, row + 1)], axis=0)
        msg_ref[MSG_NOISE + 2 * at * FL : MSG_NOISE + 2 * (at + 1) * FL, :] = pair.astype(BF16)
    live = iota((1, COLS), 1) < count_ref[0, 0]
    cell = (row_ref[...] * FL + step_ref[...] * 2).astype(F32)
    cell = jnp.where(live, cell, NO_CELL)
    val = val_ref[...]
    high = val.astype(BF16).astype(F32)
    middle = (val - high).astype(BF16).astype(F32)
    low = val - high - middle
    which = iota((16, COLS), 0)
    table = jnp.zeros((16, COLS), F32)
    for at, line in enumerate((cell, col_ref[...].astype(F32), high, middle, low)):
        table = jnp.where(which == at, line, table)
    msg_ref[MSG_OBS : MSG_OBS + 16, :] = table.astype(BF16)


def weights_kernel(conv_in_ref, conv_out_ref, embed_ref, w1_ref, w2_ref, wide_ref):
    halves = [jnp.zeros((HID, 128), F32), jnp.zeros((HID, 128), F32)]
    wide_ref[...] = jnp.zeros((HID, 128), F32)
    for at in range(9):
        wide_ref[:, 0:18] = conv_in_ref[at].astype(F32)
        start = BLOCK * (at // 3) + GROUP * (at % 3)
        shifted = wide_ref[...]
        if start % 128:
            shifted = pltpu.roll(shifted, start % 128, 1)
        halves[start // 128] = halves[start // 128] + shifted
    square = iota((HID, 128), 0) == iota((HID, 128), 1)
    line = jnp.concatenate([embed_ref[...], jnp.zeros((1, 128 - HID), F32)], axis=1)
    embed = jnp.sum(jnp.where(square, line, 0.0), axis=1, keepdims=True)
    high = embed.astype(BF16).astype(F32)
    middle = (embed - high).astype(BF16).astype(F32)
    low = embed - high - middle
    lane = iota((HID, 128), 1)
    bias = jnp.where(lane == 3 * GROUP, high, 0.0)
    bias = jnp.where(lane == 3 * GROUP + 1, middle, bias)
    bias = jnp.where(lane == 3 * GROUP + 2, low, bias)
    for frame in range(FRAMES):
        left, right = halves
        if frame:
            left = pltpu.roll(left, 2 * frame, 1)
            right = pltpu.roll(right, 2 * frame, 1)
        rows = slice(frame * HID, (frame + 1) * HID)
        w1_ref[rows, 0:128] = (0.5 * (left + bias)).astype(BF16)
        w1_ref[rows, 128:256] = (0.5 * right).astype(BF16)
    odd = iota((FL, HID), 0) % 2 == 1
    parts = []
    for at in range(9):
        upper = conv_out_ref[at, 0:1, :].astype(F32)
        lower = conv_out_ref[at, 1:2, :].astype(F32)
        parts.append(jnp.where(odd, lower, upper))
    stacked = jnp.concatenate(parts, axis=0).astype(BF16)
    shape = (HID, FRAMES * HID)
    spread = jnp.where(iota(shape, 1) % HID == iota(shape, 0), 1.0, 0.0).astype(BF16)
    tiled = jnp.dot(stacked, spread, preferred_element_type=F32)
    mine = (iota(tiled.shape, 0) % FL) // 2 == iota(tiled.shape, 1) // HID
    w2_ref[...] = jnp.where(mine, tiled, 0.0).astype(BF16)


def one_hot_maps(table, first_cell, cells):
    shape = (cells, COLS)
    hit = (iota(shape, 0) + first_cell).astype(F32) == table[0:1, :]
    lines = [jnp.where(hit, 1.0, 0.0)]
    for at in (2, 3, 4):
        lines.append(jnp.where(hit, table[at : at + 1, :], 0.0))
    lhs = jnp.concatenate(lines, axis=0).astype(BF16)
    cols_hot = jnp.where(iota((COLS, COLS), 0).astype(F32) == table[1:2, :], 1.0, 0.0)
    out = lax.dot_general(
        lhs, cols_hot.astype(BF16), (((1,), (1,)), ((), ())), preferred_element_type=F32
    )
    count = out[0:cells]
    total = out[cells : 2 * cells] + out[2 * cells : 3 * cells] + out[3 * cells : 4 * cells]
    return count, total


def maps_kernel(msg_ref, up_ref, down_ref, count_ref, total_ref):
    obs = slice(MSG_OBS, MSG_OBS + 16)
    pieces = (
        (up_ref, (ROWS - 2) * FL, 2 * FL, 0),
        (msg_ref, 0, ROWS * FL, 2 * FL),
        (down_ref, 0, 2 * FL, (ROWS + 2) * FL),
    )
    for ref, first_cell, cells, at in pieces:
        count, total = one_hot_maps(ref[obs, :].astype(F32), first_cell, cells)
        count_ref[at : at + cells, :] = count
        total_ref[at : at + cells, :] = total


def fill_windows(flags_ref, core_ref, own_ref, far_ref, win_ref, rows, level):
    even = flags_ref[0] == 1
    has_prev = flags_ref[1] == 1
    has_next = flags_ref[2] == 1
    const = jnp.full((FL, COLS), level, F32)
    for row in range(0, rows, 2):
        at = slice(row * FL, (row + 2) * FL)
        core = core_ref[at, :].astype(F32)
        own = own_ref[at, :].astype(F32)
        far = far_ref[at, :].astype(F32)
        prev = jnp.where(has_prev, jnp.where(even, far, core), 0.0)
        nxt = jnp.where(has_next, jnp.where(even, core, far), 0.0)
        for sub in range(2):
            part = slice(sub * FL, (sub + 1) * FL)
            here = jnp.concatenate([prev[part], own[part], nxt[part]], axis=0)
            block = jnp.concatenate(
                [pltpu.roll(here, 1, 1), here, pltpu.roll(here, COLS - 1, 1), const], axis=0
            )
            win_ref[(row + sub) * BLOCK : (row + sub + 1) * BLOCK, :] = block.astype(BF16)
    win_ref[rows * BLOCK : rows * BLOCK + 16, :] = jnp.zeros((16, COLS), BF16)


def hidden_products(w1_ref, w2_ref, win_ref, prod_ref, hidden_rows):
    def one_row(row, carry):
        start = pl.multiple_of(row * BLOCK, 16)
        half = jnp.dot(w1_ref[...], win_ref[pl.ds(start, DEPTH), :], preferred_element_type=F32)
        hidden = (half + half * jnp.tanh(half)).astype(BF16)
        out = jnp.dot(w2_ref[...], hidden, preferred_element_type=F32)
        prod_ref[pl.ds(pl.multiple_of(row * 72, 8), 72), :] = out
        return carry

    lax.fori_loop(0, hidden_rows, one_row, 0, unroll=2)


def net_row(prod_ref, row):
    sums = []
    for col_off in range(3):
        acc = None
        for row_off in range(3):
            at = (row + row_off) * 72 + (3 * row_off + col_off) * FL
            term = prod_ref[at : at + FL, :]
            acc = term if acc is None else acc + term
        sums.append(acc)
    return pltpu.roll(sums[0], 1, 1) + sums[1] + pltpu.roll(sums[2], COLS - 1, 1)


def advance(x, noise, net, count, total, index):
    level, after = LEVELS[index], LEVELS[index + 1]
    spread = level**2 - after**2
    denoised = x * (1.0 / (1.0 + level**2)) + (level / (1.0 + level**2) ** 0.5) * net
    guide = (total - count * denoised) * (1.0 / (OBS_NOISE + COVARIANCE_GAIN * level**2))
    score = (denoised - x) * (1.0 / level**2) + guide
    return x + spread * score + spread**0.5 * noise


def first_kernel(
    flags_ref, x_in, noise_in, up_ref, down_ref, core_ref, own_ref, far_ref, w1_ref, w2_ref,
    count_ref, total_ref, next_ref, send_ref, win_ref, prod_ref, x_ref, noise_ref,
):
    rows = 2 * ROWS
    split_halves(x_in, x_ref)
    split_halves(noise_in, noise_ref)
    fill_windows(flags_ref, core_ref, own_ref, far_ref, win_ref, rows, LEVELS[0])
    hidden_products(w1_ref, w2_ref, win_ref, prod_ref, rows - 2)
    grow = (1.0 + LEVELS[0] ** 2) ** 0.5
    shrink = 1.0 / (1.0 + LEVELS[1] ** 2) ** 0.5
    for row in range(0, ROWS + 4, 2):
        both = []
        if row == 0:
            x_pair = up_ref[(ROWS - 2) * FL : ROWS * FL, :].astype(F32) * grow
            noise_pair = up_ref[MSG_NOISE + 2 * FL : MSG_NOISE + 4 * FL, :].astype(F32)
        elif row == ROWS + 2:
            x_pair = down_ref[0 : 2 * FL, :].astype(F32) * grow
            noise_pair = down_ref[MSG_NOISE : MSG_NOISE + 2 * FL, :].astype(F32)
        for sub in range(2):
            part = slice(sub * FL, (sub + 1) * FL)
            here = row + sub
            inside = 2 <= here < ROWS + 2
            x = row_of(x_ref, here - 2) if inside else x_pair[part]
            noise = row_of(noise_ref, here - 2) if inside else noise_pair[part]
            at = slice(here * FL, (here + 1) * FL)
            new = advance(
                x, noise, net_row(prod_ref, here), count_ref[at, :], total_ref[at, :], 0
            )
            if inside:
                next_ref[(here - 2) * FL : (here - 1) * FL, :] = new
            both.append(new)
        pair = jnp.concatenate(both, axis=0) * shrink
        send_ref[row * FL : (row + 2) * FL, :] = pair.astype(BF16)


def second_kernel(
    flags_ref, x_ref, noise_in, core_ref, own_ref, far_ref, w1_ref, w2_ref,
    count_ref, total_ref, out_ref, win_ref, prod_ref, noise_ref, half_ref,
):
    rows = ROWS + 4
    split_halves(noise_in, noise_ref)
    fill_windows(flags_ref, core_ref, own_ref, far_ref, win_ref, rows, LEVELS[1])
    hidden_products(w1_ref, w2_ref, win_ref, prod_ref, rows - 2)
    for row in range(ROWS):
        at = slice((row + 2) * FL, (row + 3) * FL)
        new = advance(
            x_ref[row * FL : (row + 1) * FL, :], row_of(noise_ref, row), net_row(prod_ref, row),
            count_ref[at, :], total_ref[at, :], 1,
        )
        half_ref[pl.ds(row, FL, stride=ROWS), :] = new[:, 0:128]
        half_ref[pl.ds(ROWS * FL + row, FL, stride=ROWS), :] = new[:, 128:256]
    out_ref[:, 0:128] = half_ref[0 : ROWS * FL, :]
    out_ref[:, 128:256] = half_ref[ROWS * FL :, :]


def call(kernel, args, specs, outs, scratch=(), name=None, flops=0):
    moved = sum(a.size * a.dtype.itemsize for a in args)
    moved += sum(o.size * o.dtype.itemsize for o in outs)
    return pl.pallas_call(
        kernel,
        out_shape=tuple(outs),
        in_specs=specs,
        out_specs=tuple([VMEM] * len(outs)),
        scratch_shapes=list(scratch),
        compiler_params=params(),
        cost_estimate=pl.CostEstimate(flops=flops, bytes_accessed=moved, transcendentals=0),
        name=name,
    )(*args)


def time_pairs(n_tm, n_rows):
    core, far = [], []
    at = lambda i, r: i * n_rows + r
    for r in range(n_rows):
        for i in range(0, n_tm, 2):
            core += [(at(i, r), at(i + 1, r)), (at(i + 1, r), at(i, r))]
        for i in range(1, n_tm - 1, 2):
            far += [(at(i, r), at(i + 1, r)), (at(i + 1, r), at(i, r))]
        for i in (0, n_tm - 1):
            far.append((at(i, r), at(i, r ^ 1)))
    return core, far


def exchange_time(block, n_tm, n_rows):
    core, far = time_pairs(n_tm, n_rows)
    return (
        lax.ppermute(block, ("tm", "rows"), core),
        lax.ppermute(block, ("tm", "rows"), far),
    )


def per_device(
    noisy_states, noise_first, noise_second, conv_in, conv_out, level_embed,
    obs_count, obs_step, obs_row, obs_col, obs_value,
):
    n_tm, n_rows = lax.axis_size("tm"), lax.axis_size("rows")
    frames, layers, rows, cols = noisy_states.shape
    assert frames == FRAMES and frames * layers == FL and rows == ROWS and cols == COLS
    assert n_tm % 2 == 0 and n_rows % 2 == 0 and obs_step.shape[-1] == COLS
    flat = lambda a: a.reshape(FL * ROWS, COLS)
    line = lambda a: a.reshape(1, -1)
    x, noise_a, noise_b = flat(noisy_states), flat(noise_first), flat(noise_second)
    shape = jax.ShapeDtypeStruct
    here = lax.axis_index("tm")
    flags = jnp.stack(
        [
            (here % 2 == 0).astype(jnp.int32),
            (here > 0).astype(jnp.int32),
            (here < n_tm - 1).astype(jnp.int32),
        ]
    )

    halves = pltpu.VMEM((2 * ROWS * FL, 128), F32)
    (msg,) = call(
        pack_kernel,
        (obs_count, x, noise_a, line(obs_step), line(obs_row), line(obs_col), line(obs_value)),
        [SMEM] + [VMEM] * 6,
        [shape((MSG_ROWS, COLS), BF16)],
        [halves, halves],
        name="pack",
    )
    up = lax.ppermute(msg, "rows", [(i, (i + 1) % n_rows) for i in range(n_rows)])
    if n_rows == 2:
        down = up
    else:
        down = lax.ppermute(msg, "rows", [((i + 1) % n_rows, i) for i in range(n_rows)])
    w1, w2 = call(
        weights_kernel,
        (conv_in, conv_out, line(level_embed)),
        [VMEM] * 3,
        [shape((FRAMES * HID, DEPTH), BF16), shape((72, FRAMES * HID), BF16)],
        [pltpu.VMEM((HID, 128), F32)],
        name="weights",
    )
    half = ROWS * FL // 2
    own = jnp.concatenate([up[half : 2 * half], msg[: 2 * half], down[:half]], axis=0)
    core, far = exchange_time(own, n_tm, n_rows)
    maps = shape(((ROWS + 4) * FL, COLS), F32)
    count, total = call(maps_kernel, (msg, up, down), [VMEM] * 3, [maps, maps], name="maps")
    scratch = lambda n: [
        pltpu.VMEM((n * BLOCK + 16, COLS), BF16),
        pltpu.VMEM(((n - 2) * 72, COLS), F32),
        halves,
        halves,
    ]
    current, send = call(
        first_kernel,
        (flags, x, noise_a, up, down, core, own, far, w1, w2, count, total),
        [SMEM] + [VMEM] * 11,
        [shape((ROWS * FL, COLS), F32), shape(((ROWS + 4) * FL, COLS), BF16)],
        scratch(2 * ROWS),
        name="first",
        flops=14 * 2 * 256 * 384 * (256 + 72),
    )
    core, far = exchange_time(send, n_tm, n_rows)
    (out,) = call(
        second_kernel,
        (flags, current, noise_b, core, send, far, w1, w2, count, total),
        [SMEM] + [VMEM] * 9,
        [shape((FL * ROWS, COLS), F32)],
        scratch(ROWS + 4),
        name="second",
        flops=10 * 2 * 256 * 384 * (256 + 72),
    )
    return out.reshape(noisy_states.shape)


def solution(mesh):
    states = P("tm", None, "rows", None)
    slots = P("tm", "rows", None)
    in_specs = (states, states, states, P(), P(), P(), P("tm", "rows"), slots, slots, slots, slots)
    return jax.shard_map(
        per_device, mesh=mesh, in_specs=in_specs, out_specs=states, check_vma=False
    )
```

```python
import functools

import jax
import jax.numpy as jnp
from jax import lax
from jax.experimental import pallas as pl
from jax.experimental.pallas import tpu as pltpu
from jax.sharding import PartitionSpec as P

LEVELS = (1.0, 0.5, 0.2)
OBS_NOISE = 0.1
COVARIANCE_GAIN = 0.5

FL = 8
ROWS = 8
COLS = 256
HID = 96
FRAMES = 4
GROUP = 3 * FL
BLOCK = 80
DEPTH = 256
MSG_NOISE = ROWS * FL
MSG_OBS = MSG_NOISE + 4 * FL
MSG_ROWS = MSG_OBS + 16
NO_CELL = 64.0
AHEAD, LAG2, LAG3 = 4, 3, 3
VMEM = pl.BlockSpec(memory_space=pltpu.VMEM)
SMEM = pl.BlockSpec(memory_space=pltpu.SMEM)
F32 = jnp.float32
BF16 = jnp.bfloat16


def params():
    return pltpu.CompilerParams(vmem_limit_bytes=16 * 1024 * 1024)


def iota(shape, dim):
    return lax.broadcasted_iota(jnp.int32, shape, dim)


def split_halves(ref, halves_ref):
    halves_ref[0 : ROWS * FL, :] = ref[:, 0:128].astype(F32)
    halves_ref[ROWS * FL :, :] = ref[:, 128:256].astype(F32)


def row_of(halves_ref, row):
    left = halves_ref[pl.ds(row, FL, stride=ROWS), :]
    right = halves_ref[pl.ds(ROWS * FL + row, FL, stride=ROWS), :]
    return jnp.concatenate([left, right], axis=1)


def pack_kernel(
    count_ref, scaled_in, noise_in, step_ref, row_ref, col_ref, val_ref, msg_ref, scaled_ref, noise_ref
):
    split_halves(scaled_in, scaled_ref)
    split_halves(noise_in, noise_ref)
    for row in range(0, ROWS, 2):
        pair = jnp.concatenate([row_of(scaled_ref, row), row_of(scaled_ref, row + 1)], axis=0)
        msg_ref[row * FL : (row + 2) * FL, :] = pair.astype(BF16)
    for at, row in enumerate((0, ROWS - 2)):
        pair = jnp.concatenate([row_of(noise_ref, row), row_of(noise_ref, row + 1)], axis=0)
        msg_ref[MSG_NOISE + 2 * at * FL : MSG_NOISE + 2 * (at + 1) * FL, :] = pair.astype(BF16)
    live = iota((1, COLS), 1) < count_ref[0, 0]
    cell = (row_ref[...] * FL + step_ref[...] * 2).astype(F32)
    cell = jnp.where(live, cell, NO_CELL)
    val = val_ref[...]
    high = val.astype(BF16).astype(F32)
    middle = (val - high).astype(BF16).astype(F32)
    low = val - high - middle
    which = iota((16, COLS), 0)
    table = jnp.zeros((16, COLS), F32)
    for at, line in enumerate((cell, col_ref[...].astype(F32), high, middle, low)):
        table = jnp.where(which == at, line, table)
    msg_ref[MSG_OBS : MSG_OBS + 16, :] = table.astype(BF16)


def weights_kernel(conv_in_ref, conv_out_ref, embed_ref, w1_ref, w2_ref, wide_ref):
    halves = [jnp.zeros((HID, 128), F32), jnp.zeros((HID, 128), F32)]
    wide_ref[...] = jnp.zeros((HID, 128), F32)
    for at in range(9):
        wide_ref[:, 0:18] = conv_in_ref[at].astype(F32)
        start = BLOCK * (at // 3) + GROUP * (at % 3)
        shifted = wide_ref[...]
        if start % 128:
            shifted = pltpu.roll(shifted, start % 128, 1)
        halves[start // 128] = halves[start // 128] + shifted
    square = iota((HID, 128), 0) == iota((HID, 128), 1)
    line = jnp.concatenate([embed_ref[...], jnp.zeros((1, 128 - HID), F32)], axis=1)
    embed = jnp.sum(jnp.where(square, line, 0.0), axis=1, keepdims=True)
    high = embed.astype(BF16).astype(F32)
    middle = (embed - high).astype(BF16).astype(F32)
    low = embed - high - middle
    lane = iota((HID, 128), 1)
    bias = jnp.where(lane == 3 * GROUP, high, 0.0)
    bias = jnp.where(lane == 3 * GROUP + 1, middle, bias)
    bias = jnp.where(lane == 3 * GROUP + 2, low, bias)
    for frame in range(FRAMES):
        left, right = halves
        if frame:
            left = pltpu.roll(left, 2 * frame, 1)
            right = pltpu.roll(right, 2 * frame, 1)
        rows = slice(frame * HID, (frame + 1) * HID)
        w1_ref[rows, 0:128] = (0.5 * (left + bias)).astype(BF16)
        w1_ref[rows, 128:256] = (0.5 * right).astype(BF16)
    odd = iota((FL, HID), 0) % 2 == 1
    parts = []
    for at in range(9):
        upper = conv_out_ref[at, 0:1, :].astype(F32)
        lower = conv_out_ref[at, 1:2, :].astype(F32)
        parts.append(jnp.where(odd, lower, upper))
    stacked = jnp.concatenate(parts, axis=0).astype(BF16)
    shape = (HID, FRAMES * HID)
    spread = jnp.where(iota(shape, 1) % HID == iota(shape, 0), 1.0, 0.0).astype(BF16)
    tiled = jnp.dot(stacked, spread, preferred_element_type=F32)
    mine = (iota(tiled.shape, 0) % FL) // 2 == iota(tiled.shape, 1) // HID
    w2_ref[...] = jnp.where(mine, tiled, 0.0).astype(BF16)


def one_hot_maps(table, first_cell, cells):
    shape = (cells, COLS)
    hit = (iota(shape, 0) + first_cell).astype(F32) == table[0:1, :]
    lines = [jnp.where(hit, 1.0, 0.0)]
    for at in (2, 3, 4):
        lines.append(jnp.where(hit, table[at : at + 1, :], 0.0))
    lhs = jnp.concatenate(lines, axis=0).astype(BF16)
    cols_hot = jnp.where(iota((COLS, COLS), 0).astype(F32) == table[1:2, :], 1.0, 0.0)
    out = lax.dot_general(
        lhs, cols_hot.astype(BF16), (((1,), (1,)), ((), ())), preferred_element_type=F32
    )
    count = out[0:cells]
    total = out[cells : 2 * cells] + out[2 * cells : 3 * cells] + out[3 * cells : 4 * cells]
    return count, total


def maps_kernel(msg_ref, up_ref, down_ref, count_ref, total_ref):
    obs = slice(MSG_OBS, MSG_OBS + 16)
    pieces = (
        (up_ref, (ROWS - 2) * FL, 2 * FL, 0),
        (msg_ref, 0, ROWS * FL, 2 * FL),
        (down_ref, 0, 2 * FL, (ROWS + 2) * FL),
    )
    for ref, first_cell, cells, at in pieces:
        count, total = one_hot_maps(ref[obs, :].astype(F32), first_cell, cells)
        count_ref[at : at + cells, :] = count
        total_ref[at : at + cells, :] = total


def fill_pair(flags, refs, win_ref, pair, level):
    even, has_prev, has_next = flags
    at = slice(2 * pair * FL, 2 * (pair + 1) * FL)
    core, own, far = (ref[at, :].astype(F32) for ref in refs)
    prev = jnp.where(has_prev, jnp.where(even, far, core), 0.0)
    nxt = jnp.where(has_next, jnp.where(even, core, far), 0.0)
    const = jnp.full((FL, COLS), level, F32)
    for sub in range(2):
        part = slice(sub * FL, (sub + 1) * FL)
        here = jnp.concatenate([prev[part], own[part], nxt[part]], axis=0)
        block = jnp.concatenate(
            [pltpu.roll(here, 1, 1), here, pltpu.roll(here, COLS - 1, 1), const], axis=0
        )
        start = (2 * pair + sub) * BLOCK
        win_ref[start : start + BLOCK, :] = block.astype(BF16)


def run_rows(flags_ref, refs, w1_ref, w2_ref, win_ref, hid_ref, prod_ref, rows, level, emit):
    flags = [flags_ref[at] == 1 for at in range(3)]
    hidden_rows = rows - 2
    n = FRAMES * HID
    win_ref[rows * BLOCK : rows * BLOCK + 16, :] = jnp.zeros((16, COLS), BF16)
    filled = 0
    for step in range(hidden_rows + LAG2 + LAG3):
        want = min(rows, step + 3 + AHEAD)
        while 2 * filled < want:
            fill_pair(flags, refs, win_ref, filled, level)
            filled += 1
        if step < hidden_rows:
            start = step * BLOCK
            half = jnp.dot(w1_ref[...], win_ref[start : start + DEPTH, :], preferred_element_type=F32)
            hid_ref[step * n : (step + 1) * n, :] = (half + half * jnp.tanh(half)).astype(BF16)
        row = step - LAG2
        if 0 <= row < hidden_rows:
            prod_ref[row * 72 : (row + 1) * 72, :] = jnp.dot(
                w2_ref[...], hid_ref[row * n : (row + 1) * n, :], preferred_element_type=F32
            )
        row = step - LAG2 - LAG3
        if row >= 2:
            emit(row - 2)


def net_row(prod_ref, row):
    sums = []
    for col_off in range(3):
        acc = None
        for row_off in range(3):
            at = (row + row_off) * 72 + (3 * row_off + col_off) * FL
            term = prod_ref[at : at + FL, :]
            acc = term if acc is None else acc + term
        sums.append(acc)
    return pltpu.roll(sums[0], 1, 1) + sums[1] + pltpu.roll(sums[2], COLS - 1, 1)


def advance(x, noise, net, count, total, index):
    level, after = LEVELS[index], LEVELS[index + 1]
    spread = level**2 - after**2
    denoised = x * (1.0 / (1.0 + level**2)) + (level / (1.0 + level**2) ** 0.5) * net
    guide = (total - count * denoised) * (1.0 / (OBS_NOISE + COVARIANCE_GAIN * level**2))
    score = (denoised - x) * (1.0 / level**2) + guide
    return x + spread * score + spread**0.5 * noise


def first_kernel(
    flags_ref, x_in, noise_in, up_ref, down_ref, core_ref, own_ref, far_ref, w1_ref, w2_ref,
    count_ref, total_ref, next_ref, send_ref, win_ref, hid_ref, prod_ref, x_ref, noise_ref,
):
    split_halves(x_in, x_ref)
    split_halves(noise_in, noise_ref)
    grow = (1.0 + LEVELS[0] ** 2) ** 0.5
    shrink = 1.0 / (1.0 + LEVELS[1] ** 2) ** 0.5
    made = {}

    def emit(here):
        part = slice((here % 2) * FL, (here % 2 + 1) * FL)
        if here < 2:
            x = up_ref[(ROWS - 2) * FL : ROWS * FL, :].astype(F32)[part] * grow
            noise = up_ref[MSG_NOISE + 2 * FL : MSG_NOISE + 4 * FL, :].astype(F32)[part]
        elif here >= ROWS + 2:
            x = down_ref[0 : 2 * FL, :].astype(F32)[part] * grow
            noise = down_ref[MSG_NOISE : MSG_NOISE + 2 * FL, :].astype(F32)[part]
        else:
            x, noise = row_of(x_ref, here - 2), row_of(noise_ref, here - 2)
        at = slice(here * FL, (here + 1) * FL)
        new = advance(x, noise, net_row(prod_ref, here), count_ref[at, :], total_ref[at, :], 0)
        if 2 <= here < ROWS + 2:
            next_ref[(here - 2) * FL : (here - 1) * FL, :] = new
        made[here % 2] = new
        if here % 2:
            pair = jnp.concatenate([made[0], made[1]], axis=0) * shrink
            send_ref[(here - 1) * FL : (here + 1) * FL, :] = pair.astype(BF16)

    run_rows(
        flags_ref, (core_ref, own_ref, far_ref), w1_ref, w2_ref, win_ref, hid_ref, prod_ref,
        2 * ROWS, LEVELS[0], emit,
    )


def second_kernel(
    flags_ref, x_ref, noise_in, core_ref, own_ref, far_ref, w1_ref, w2_ref,
    count_ref, total_ref, out_ref, win_ref, hid_ref, prod_ref, noise_ref, half_ref,
):
    split_halves(noise_in, noise_ref)

    def emit(row):
        at = slice((row + 2) * FL, (row + 3) * FL)
        new = advance(
            x_ref[row * FL : (row + 1) * FL, :], row_of(noise_ref, row), net_row(prod_ref, row),
            count_ref[at, :], total_ref[at, :], 1,
        )
        half_ref[pl.ds(row, FL, stride=ROWS), :] = new[:, 0:128]
        half_ref[pl.ds(ROWS * FL + row, FL, stride=ROWS), :] = new[:, 128:256]

    run_rows(
        flags_ref, (core_ref, own_ref, far_ref), w1_ref, w2_ref, win_ref, hid_ref, prod_ref,
        ROWS + 4, LEVELS[1], emit,
    )
    out_ref[:, 0:128] = half_ref[0 : ROWS * FL, :]
    out_ref[:, 128:256] = half_ref[ROWS * FL :, :]


def call(kernel, args, specs, outs, scratch=(), name=None, flops=0):
    moved = sum(a.size * a.dtype.itemsize for a in args)
    moved += sum(o.size * o.dtype.itemsize for o in outs)
    return pl.pallas_call(
        kernel,
        out_shape=tuple(outs),
        in_specs=specs,
        out_specs=tuple([VMEM] * len(outs)),
        scratch_shapes=list(scratch),
        compiler_params=params(),
        cost_estimate=pl.CostEstimate(flops=flops, bytes_accessed=moved, transcendentals=0),
        name=name,
    )(*args)


def time_pairs(n_tm, n_rows):
    core, far = [], []
    at = lambda i, r: i * n_rows + r
    for r in range(n_rows):
        for i in range(0, n_tm, 2):
            core += [(at(i, r), at(i + 1, r)), (at(i + 1, r), at(i, r))]
        for i in range(1, n_tm - 1, 2):
            far += [(at(i, r), at(i + 1, r)), (at(i + 1, r), at(i, r))]
        for i in (0, n_tm - 1):
            far.append((at(i, r), at(i, r ^ 1)))
    return core, far


def exchange_time(block, n_tm, n_rows):
    core, far = time_pairs(n_tm, n_rows)
    return (
        lax.ppermute(block, ("tm", "rows"), core),
        lax.ppermute(block, ("tm", "rows"), far),
    )


def scratch_for(rows):
    halves = pltpu.VMEM((2 * ROWS * FL, 128), F32)
    return [
        pltpu.VMEM((rows * BLOCK + 16, COLS), BF16),
        pltpu.VMEM(((rows - 2) * FRAMES * HID, COLS), BF16),
        pltpu.VMEM(((rows - 2) * 72, COLS), F32),
        halves,
        halves,
    ]


def first_call(*args):
    shape = jax.ShapeDtypeStruct
    return call(
        first_kernel,
        args,
        [SMEM] + [VMEM] * 11,
        [shape((ROWS * FL, COLS), F32), shape(((ROWS + 4) * FL, COLS), BF16)],
        scratch_for(2 * ROWS),
        name="first",
        flops=14 * 2 * 256 * 384 * (256 + 72),
    )


def second_call(*args):
    (out,) = call(
        second_kernel,
        args,
        [SMEM] + [VMEM] * 9,
        [jax.ShapeDtypeStruct((FL * ROWS, COLS), F32)],
        scratch_for(ROWS + 4),
        name="second",
        flops=10 * 2 * 256 * 384 * (256 + 72),
    )
    return out


def per_device(
    noisy_states, noise_first, noise_second, conv_in, conv_out, level_embed,
    obs_count, obs_step, obs_row, obs_col, obs_value,
):
    n_tm, n_rows = lax.axis_size("tm"), lax.axis_size("rows")
    frames, layers, rows, cols = noisy_states.shape
    assert frames == FRAMES and frames * layers == FL and rows == ROWS and cols == COLS
    assert n_tm % 2 == 0 and n_rows % 2 == 0 and obs_step.shape[-1] == COLS
    flat = lambda a: a.reshape(FL * ROWS, COLS)
    line = lambda a: a.reshape(1, -1)
    x, noise_a, noise_b = flat(noisy_states), flat(noise_first), flat(noise_second)
    shape = jax.ShapeDtypeStruct
    here = lax.axis_index("tm")
    flags = jnp.stack(
        [
            (here % 2 == 0).astype(jnp.int32),
            (here > 0).astype(jnp.int32),
            (here < n_tm - 1).astype(jnp.int32),
        ]
    )

    scaled = (x / (1.0 + LEVELS[0] ** 2) ** 0.5).astype(BF16)
    halves = pltpu.VMEM((2 * ROWS * FL, 128), F32)
    (msg,) = call(
        pack_kernel,
        (obs_count, scaled, noise_a, line(obs_step), line(obs_row), line(obs_col), line(obs_value)),
        [SMEM] + [VMEM] * 6,
        [shape((MSG_ROWS, COLS), BF16)],
        [halves, halves],
        name="pack",
    )
    up = lax.ppermute(msg, "rows", [(i, (i + 1) % n_rows) for i in range(n_rows)])
    if n_rows == 2:
        down = up
    else:
        down = lax.ppermute(msg, "rows", [((i + 1) % n_rows, i) for i in range(n_rows)])
    w1, w2 = call(
        weights_kernel,
        (conv_in, conv_out, line(level_embed)),
        [VMEM] * 3,
        [shape((FRAMES * HID, DEPTH), BF16), shape((72, FRAMES * HID), BF16)],
        [pltpu.VMEM((HID, 128), F32)],
        name="weights",
    )
    half = ROWS * FL // 2
    own = jnp.concatenate([up[half : 2 * half], msg[: 2 * half], down[:half]], axis=0)
    core, far = exchange_time(own, n_tm, n_rows)
    maps = shape(((ROWS + 4) * FL, COLS), F32)
    count, total = call(maps_kernel, (msg, up, down), [VMEM] * 3, [maps, maps], name="maps")
    current, send = first_call(
        flags, x, noise_a, up, down, core, own, far, w1, w2, count, total
    )
    core, far = exchange_time(send, n_tm, n_rows)
    out = second_call(flags, current, noise_b, core, send, far, w1, w2, count, total)
    return out.reshape(noisy_states.shape)


def solution(mesh):
    states = P("tm", None, "rows", None)
    slots = P("tm", "rows", None)
    in_specs = (states, states, states, P(), P(), P(), P("tm", "rows"), slots, slots, slots, slots)
    return jax.shard_map(
        per_device, mesh=mesh, in_specs=in_specs, out_specs=states, check_vma=False
    )
```

```python
import functools

import jax
import jax.numpy as jnp
from jax import lax
from jax.experimental import pallas as pl
from jax.experimental.pallas import tpu as pltpu
from jax.sharding import PartitionSpec as P

LEVELS = (1.0, 0.5, 0.2)
OBS_NOISE = 0.1
COVARIANCE_GAIN = 0.5

FL = 8
ROWS = 8
COLS = 256
HID = 96
FRAMES = 4
GROUP = 3 * FL
BLOCK = 80
DEPTH = 256
AUX_OBS = 4 * FL
AUX_ROWS = AUX_OBS + 16
NO_CELL = 64.0
AHEAD, LAG2, LAG3 = 4, 3, 3
VMEM = pl.BlockSpec(memory_space=pltpu.VMEM)
SMEM = pl.BlockSpec(memory_space=pltpu.SMEM)
F32 = jnp.float32
BF16 = jnp.bfloat16


def params():
    return pltpu.CompilerParams(vmem_limit_bytes=16 * 1024 * 1024)


def iota(shape, dim):
    return lax.broadcasted_iota(jnp.int32, shape, dim)


def split_halves(ref, halves_ref):
    halves_ref[0 : ROWS * FL, :] = ref[:, 0:128].astype(F32)
    halves_ref[ROWS * FL :, :] = ref[:, 128:256].astype(F32)


def row_of(halves_ref, row):
    left = halves_ref[pl.ds(row, FL, stride=ROWS), :]
    right = halves_ref[pl.ds(ROWS * FL + row, FL, stride=ROWS), :]
    return jnp.concatenate([left, right], axis=1)


def pack_kernel(scaled_in, msg_ref, scaled_ref):
    split_halves(scaled_in, scaled_ref)
    for row in range(0, ROWS, 2):
        pair = jnp.concatenate([row_of(scaled_ref, row), row_of(scaled_ref, row + 1)], axis=0)
        msg_ref[row * FL : (row + 2) * FL, :] = pair.astype(BF16)


def aux_kernel(count_ref, noise_in, step_ref, row_ref, col_ref, val_ref, aux_ref, noise_ref):
    split_halves(noise_in, noise_ref)
    for at, row in enumerate((0, ROWS - 2)):
        pair = jnp.concatenate([row_of(noise_ref, row), row_of(noise_ref, row + 1)], axis=0)
        aux_ref[2 * at * FL : 2 * (at + 1) * FL, :] = pair.astype(BF16)
    live = iota((1, COLS), 1) < count_ref[0, 0]
    cell = (row_ref[...] * FL + step_ref[...] * 2).astype(F32)
    cell = jnp.where(live, cell, NO_CELL)
    val = val_ref[...]
    high = val.astype(BF16).astype(F32)
    middle = (val - high).astype(BF16).astype(F32)
    low = val - high - middle
    which = iota((16, COLS), 0)
    table = jnp.zeros((16, COLS), F32)
    for at, line in enumerate((cell, col_ref[...].astype(F32), high, middle, low)):
        table = jnp.where(which == at, line, table)
    aux_ref[AUX_OBS:AUX_ROWS, :] = table.astype(BF16)


def weights_kernel(conv_in_ref, conv_out_ref, embed_ref, w1_ref, w2_ref, wide_ref):
    halves = [jnp.zeros((HID, 128), F32), jnp.zeros((HID, 128), F32)]
    wide_ref[...] = jnp.zeros((HID, 128), F32)
    for at in range(9):
        wide_ref[:, 0:18] = conv_in_ref[at].astype(F32)
        start = BLOCK * (at // 3) + GROUP * (at % 3)
        shifted = wide_ref[...]
        if start % 128:
            shifted = pltpu.roll(shifted, start % 128, 1)
        halves[start // 128] = halves[start // 128] + shifted
    square = iota((HID, 128), 0) == iota((HID, 128), 1)
    line = jnp.concatenate([embed_ref[...], jnp.zeros((1, 128 - HID), F32)], axis=1)
    embed = jnp.sum(jnp.where(square, line, 0.0), axis=1, keepdims=True)
    high = embed.astype(BF16).astype(F32)
    middle = (embed - high).astype(BF16).astype(F32)
    low = embed - high - middle
    lane = iota((HID, 128), 1)
    bias = jnp.where(lane == 3 * GROUP, high, 0.0)
    bias = jnp.where(lane == 3 * GROUP + 1, middle, bias)
    bias = jnp.where(lane == 3 * GROUP + 2, low, bias)
    for frame in range(FRAMES):
        left, right = halves
        if frame:
            left = pltpu.roll(left, 2 * frame, 1)
            right = pltpu.roll(right, 2 * frame, 1)
        rows = slice(frame * HID, (frame + 1) * HID)
        w1_ref[rows, 0:128] = (0.5 * (left + bias)).astype(BF16)
        w1_ref[rows, 128:256] = (0.5 * right).astype(BF16)
    odd = iota((FL, HID), 0) % 2 == 1
    parts = []
    for at in range(9):
        upper = conv_out_ref[at, 0:1, :].astype(F32)
        lower = conv_out_ref[at, 1:2, :].astype(F32)
        parts.append(jnp.where(odd, lower, upper))
    stacked = jnp.concatenate(parts, axis=0).astype(BF16)
    shape = (HID, FRAMES * HID)
    spread = jnp.where(iota(shape, 1) % HID == iota(shape, 0), 1.0, 0.0).astype(BF16)
    tiled = jnp.dot(stacked, spread, preferred_element_type=F32)
    mine = (iota(tiled.shape, 0) % FL) // 2 == iota(tiled.shape, 1) // HID
    w2_ref[...] = jnp.where(mine, tiled, 0.0).astype(BF16)


def one_hot_maps(table, first_cell, cells):
    shape = (cells, COLS)
    hit = (iota(shape, 0) + first_cell).astype(F32) == table[0:1, :]
    lines = [jnp.where(hit, 1.0, 0.0)]
    for at in (2, 3, 4):
        lines.append(jnp.where(hit, table[at : at + 1, :], 0.0))
    lhs = jnp.concatenate(lines, axis=0).astype(BF16)
    cols_hot = jnp.where(iota((COLS, COLS), 0).astype(F32) == table[1:2, :], 1.0, 0.0)
    out = lax.dot_general(
        lhs, cols_hot.astype(BF16), (((1,), (1,)), ((), ())), preferred_element_type=F32
    )
    count = out[0:cells]
    total = out[cells : 2 * cells] + out[2 * cells : 3 * cells] + out[3 * cells : 4 * cells]
    return count, total


def maps_kernel(msg_ref, up_ref, down_ref, count_ref, total_ref):
    obs = slice(AUX_OBS, AUX_ROWS)
    pieces = (
        (up_ref, (ROWS - 2) * FL, 2 * FL, 0),
        (msg_ref, 0, ROWS * FL, 2 * FL),
        (down_ref, 0, 2 * FL, (ROWS + 2) * FL),
    )
    for ref, first_cell, cells, at in pieces:
        count, total = one_hot_maps(ref[obs, :].astype(F32), first_cell, cells)
        count_ref[at : at + cells, :] = count
        total_ref[at : at + cells, :] = total


def fill_pair(flags, refs, win_ref, pair, level):
    even, has_prev, has_next = flags
    at = slice(2 * pair * FL, 2 * (pair + 1) * FL)
    core, own, far = (ref[at, :].astype(F32) for ref in refs)
    prev = jnp.where(has_prev, jnp.where(even, far, core), 0.0)
    nxt = jnp.where(has_next, jnp.where(even, core, far), 0.0)
    const = jnp.full((FL, COLS), level, F32)
    for sub in range(2):
        part = slice(sub * FL, (sub + 1) * FL)
        here = jnp.concatenate([prev[part], own[part], nxt[part]], axis=0)
        block = jnp.concatenate(
            [pltpu.roll(here, 1, 1), here, pltpu.roll(here, COLS - 1, 1), const], axis=0
        )
        start = (2 * pair + sub) * BLOCK
        win_ref[start : start + BLOCK, :] = block.astype(BF16)


def run_rows(flags_ref, refs, w1_ref, w2_ref, win_ref, hid_ref, prod_ref, rows, level, emit):
    flags = [flags_ref[at] == 1 for at in range(3)]
    hidden_rows = rows - 2
    n = FRAMES * HID
    win_ref[rows * BLOCK : rows * BLOCK + 16, :] = jnp.zeros((16, COLS), BF16)
    filled = 0
    for step in range(hidden_rows + LAG2 + LAG3):
        want = min(rows, step + 3 + AHEAD)
        while 2 * filled < want:
            fill_pair(flags, refs, win_ref, filled, level)
            filled += 1
        if step < hidden_rows:
            start = step * BLOCK
            half = jnp.dot(w1_ref[...], win_ref[start : start + DEPTH, :], preferred_element_type=F32)
            hid_ref[step * n : (step + 1) * n, :] = (half + half * jnp.tanh(half)).astype(BF16)
        row = step - LAG2
        if 0 <= row < hidden_rows:
            prod_ref[row * 72 : (row + 1) * 72, :] = jnp.dot(
                w2_ref[...], hid_ref[row * n : (row + 1) * n, :], preferred_element_type=F32
            )
        row = step - LAG2 - LAG3
        if row >= 2:
            emit(row - 2)


def net_row(prod_ref, row):
    sums = []
    for col_off in range(3):
        acc = None
        for row_off in range(3):
            at = (row + row_off) * 72 + (3 * row_off + col_off) * FL
            term = prod_ref[at : at + FL, :]
            acc = term if acc is None else acc + term
        sums.append(acc)
    return pltpu.roll(sums[0], 1, 1) + sums[1] + pltpu.roll(sums[2], COLS - 1, 1)


def advance(x, noise, net, count, total, index):
    level, after = LEVELS[index], LEVELS[index + 1]
    spread = level**2 - after**2
    denoised = x * (1.0 / (1.0 + level**2)) + (level / (1.0 + level**2) ** 0.5) * net
    guide = (total - count * denoised) * (1.0 / (OBS_NOISE + COVARIANCE_GAIN * level**2))
    score = (denoised - x) * (1.0 / level**2) + guide
    return x + spread * score + spread**0.5 * noise


def first_kernel(
    flags_ref, x_in, noise_in, aux_up_ref, aux_down_ref, core_ref, own_ref, far_ref, w1_ref,
    w2_ref, count_ref, total_ref, next_ref, send_ref, win_ref, hid_ref, prod_ref, x_ref, noise_ref,
):
    split_halves(x_in, x_ref)
    split_halves(noise_in, noise_ref)
    grow = (1.0 + LEVELS[0] ** 2) ** 0.5
    shrink = 1.0 / (1.0 + LEVELS[1] ** 2) ** 0.5
    made = {}

    def emit(here):
        part = slice((here % 2) * FL, (here % 2 + 1) * FL)
        if not 2 <= here < ROWS + 2:
            at = (here + 2) // 2 * 2 * FL
            x = own_ref[at : at + 2 * FL, :].astype(F32)[part] * grow
            ref, start = (aux_up_ref, 2 * FL) if here < 2 else (aux_down_ref, 0)
            noise = ref[start : start + 2 * FL, :].astype(F32)[part]
        else:
            x, noise = row_of(x_ref, here - 2), row_of(noise_ref, here - 2)
        at = slice(here * FL, (here + 1) * FL)
        new = advance(x, noise, net_row(prod_ref, here), count_ref[at, :], total_ref[at, :], 0)
        if 2 <= here < ROWS + 2:
            next_ref[(here - 2) * FL : (here - 1) * FL, :] = new
        made[here % 2] = new
        if here % 2:
            pair = jnp.concatenate([made[0], made[1]], axis=0) * shrink
            send_ref[(here - 1) * FL : (here + 1) * FL, :] = pair.astype(BF16)

    run_rows(
        flags_ref, (core_ref, own_ref, far_ref), w1_ref, w2_ref, win_ref, hid_ref, prod_ref,
        2 * ROWS, LEVELS[0], emit,
    )


def second_kernel(
    flags_ref, x_ref, noise_in, core_ref, own_ref, far_ref, w1_ref, w2_ref,
    count_ref, total_ref, out_ref, win_ref, hid_ref, prod_ref, noise_ref, half_ref,
):
    split_halves(noise_in, noise_ref)

    def emit(row):
        at = slice((row + 2) * FL, (row + 3) * FL)
        new = advance(
            x_ref[row * FL : (row + 1) * FL, :], row_of(noise_ref, row), net_row(prod_ref, row),
            count_ref[at, :], total_ref[at, :], 1,
        )
        half_ref[pl.ds(row, FL, stride=ROWS), :] = new[:, 0:128]
        half_ref[pl.ds(ROWS * FL + row, FL, stride=ROWS), :] = new[:, 128:256]

    run_rows(
        flags_ref, (core_ref, own_ref, far_ref), w1_ref, w2_ref, win_ref, hid_ref, prod_ref,
        ROWS + 4, LEVELS[1], emit,
    )
    out_ref[:, 0:128] = half_ref[0 : ROWS * FL, :]
    out_ref[:, 128:256] = half_ref[ROWS * FL :, :]


def call(kernel, args, specs, outs, scratch=(), name=None, flops=0):
    moved = sum(a.size * a.dtype.itemsize for a in args)
    moved += sum(o.size * o.dtype.itemsize for o in outs)
    return pl.pallas_call(
        kernel,
        out_shape=tuple(outs),
        in_specs=specs,
        out_specs=tuple([VMEM] * len(outs)),
        scratch_shapes=list(scratch),
        compiler_params=params(),
        cost_estimate=pl.CostEstimate(flops=flops, bytes_accessed=moved, transcendentals=0),
        name=name,
    )(*args)


def time_pairs(n_tm, n_rows):
    core, far = [], []
    at = lambda i, r: i * n_rows + r
    for r in range(n_rows):
        for i in range(0, n_tm, 2):
            core += [(at(i, r), at(i + 1, r)), (at(i + 1, r), at(i, r))]
        for i in range(1, n_tm - 1, 2):
            far += [(at(i, r), at(i + 1, r)), (at(i + 1, r), at(i, r))]
        for i in (0, n_tm - 1):
            far.append((at(i, r), at(i, r ^ 1)))
    return core, far


def exchange_rows(block, n_rows):
    up = lax.ppermute(block, "rows", [(i, (i + 1) % n_rows) for i in range(n_rows)])
    if n_rows == 2:
        return up, up
    return up, lax.ppermute(block, "rows", [((i + 1) % n_rows, i) for i in range(n_rows)])


def exchange_time(block, n_tm, n_rows):
    core, far = time_pairs(n_tm, n_rows)
    return (
        lax.ppermute(block, ("tm", "rows"), core),
        lax.ppermute(block, ("tm", "rows"), far),
    )


def scratch_for(rows):
    halves = pltpu.VMEM((2 * ROWS * FL, 128), F32)
    return [
        pltpu.VMEM((rows * BLOCK + 16, COLS), BF16),
        pltpu.VMEM(((rows - 2) * FRAMES * HID, COLS), BF16),
        pltpu.VMEM(((rows - 2) * 72, COLS), F32),
        halves,
        halves,
    ]


def first_call(*args):
    shape = jax.ShapeDtypeStruct
    return call(
        first_kernel,
        args,
        [SMEM] + [VMEM] * 11,
        [shape((ROWS * FL, COLS), F32), shape(((ROWS + 4) * FL, COLS), BF16)],
        scratch_for(2 * ROWS),
        name="first",
        flops=14 * 2 * 256 * 384 * (256 + 72),
    )


def second_call(*args):
    (out,) = call(
        second_kernel,
        args,
        [SMEM] + [VMEM] * 9,
        [jax.ShapeDtypeStruct((FL * ROWS, COLS), F32)],
        scratch_for(ROWS + 4),
        name="second",
        flops=10 * 2 * 256 * 384 * (256 + 72),
    )
    return out


def per_device(
    noisy_states, noise_first, noise_second, conv_in, conv_out, level_embed,
    obs_count, obs_step, obs_row, obs_col, obs_value,
):
    n_tm, n_rows = lax.axis_size("tm"), lax.axis_size("rows")
    frames, layers, rows, cols = noisy_states.shape
    assert frames == FRAMES and frames * layers == FL and rows == ROWS and cols == COLS
    assert n_tm % 2 == 0 and n_rows % 2 == 0 and obs_step.shape[-1] == COLS
    flat = lambda a: a.reshape(FL * ROWS, COLS)
    line = lambda a: a.reshape(1, -1)
    x, noise_a, noise_b = flat(noisy_states), flat(noise_first), flat(noise_second)
    shape = jax.ShapeDtypeStruct
    here = lax.axis_index("tm")
    flags = jnp.stack(
        [
            (here % 2 == 0).astype(jnp.int32),
            (here > 0).astype(jnp.int32),
            (here < n_tm - 1).astype(jnp.int32),
        ]
    )

    scaled = (x / (1.0 + LEVELS[0] ** 2) ** 0.5).astype(BF16)
    halves = pltpu.VMEM((2 * ROWS * FL, 128), F32)
    (msg,) = call(
        pack_kernel,
        (scaled,),
        [VMEM],
        [shape((ROWS * FL, COLS), BF16)],
        [halves],
        name="pack",
    )
    (aux,) = call(
        aux_kernel,
        (obs_count, noise_a, line(obs_step), line(obs_row), line(obs_col), line(obs_value)),
        [SMEM] + [VMEM] * 5,
        [shape((AUX_ROWS, COLS), BF16)],
        [halves],
        name="aux",
    )
    up, down = exchange_rows(msg, n_rows)
    aux_up, aux_down = exchange_rows(aux, n_rows)
    w1, w2 = call(
        weights_kernel,
        (conv_in, conv_out, line(level_embed)),
        [VMEM] * 3,
        [shape((FRAMES * HID, DEPTH), BF16), shape((72, FRAMES * HID), BF16)],
        [pltpu.VMEM((HID, 128), F32)],
        name="weights",
    )
    half = ROWS * FL // 2
    own = jnp.concatenate([up[half:], msg, down[:half]], axis=0)
    core, far = exchange_time(own, n_tm, n_rows)
    maps = shape(((ROWS + 4) * FL, COLS), F32)
    count, total = call(maps_kernel, (aux, aux_up, aux_down), [VMEM] * 3, [maps, maps], name="maps")
    current, send = first_call(
        flags, x, noise_a, aux_up, aux_down, core, own, far, w1, w2, count, total
    )
    core, far = exchange_time(send, n_tm, n_rows)
    out = second_call(flags, current, noise_b, core, send, far, w1, w2, count, total)
    return out.reshape(noisy_states.shape)


def solution(mesh):
    states = P("tm", None, "rows", None)
    slots = P("tm", "rows", None)
    in_specs = (states, states, states, P(), P(), P(), P("tm", "rows"), slots, slots, slots, slots)
    return jax.shard_map(
        per_device, mesh=mesh, in_specs=in_specs, out_specs=states, check_vma=False
    )
```

```python
import jax
import jax.numpy as jnp
from jax import lax
from jax.experimental import pallas as pl
from jax.experimental.pallas import tpu as pltpu
from jax.sharding import PartitionSpec as P


LEVELS = (1.0, 0.5, 0.2)
OBS_NOISE = 0.1
COVARIANCE_GAIN = 0.5

FL = 8
ROWS = 8
COLS = 256
HID = 96
FRAMES = 4
GROUP = 3 * FL
BLOCK = 80
DEPTH = 256
AUX_OBS = 4 * FL
AUX_ROWS = AUX_OBS + 16
NO_CELL = 64.0
AHEAD, LAG2, LAG3 = 4, 3, 3
VMEM = pl.BlockSpec(memory_space=pltpu.VMEM)
SMEM = pl.BlockSpec(memory_space=pltpu.SMEM)
F32 = jnp.float32
BF16 = jnp.bfloat16


def params():
    return pltpu.CompilerParams(vmem_limit_bytes=16 * 1024 * 1024)


def iota(shape, dim):
    return lax.broadcasted_iota(jnp.int32, shape, dim)


def split_halves(ref, halves_ref):
    halves_ref[0 : ROWS * FL, :] = ref[:, 0:128].astype(F32)
    halves_ref[ROWS * FL :, :] = ref[:, 128:256].astype(F32)


def row_of(halves_ref, row):
    left = halves_ref[pl.ds(row, FL, stride=ROWS), :]
    right = halves_ref[pl.ds(ROWS * FL + row, FL, stride=ROWS), :]
    return jnp.concatenate([left, right], axis=1)


def pack_kernel(scaled_in, msg_ref, scaled_ref):
    split_halves(scaled_in, scaled_ref)
    for row in range(0, ROWS, 2):
        pair = jnp.concatenate([row_of(scaled_ref, row), row_of(scaled_ref, row + 1)], axis=0)
        msg_ref[row * FL : (row + 2) * FL, :] = pair.astype(BF16)


def aux_kernel(count_ref, noise_in, step_ref, row_ref, col_ref, val_ref, aux_ref, noise_ref):
    split_halves(noise_in, noise_ref)
    for at, row in enumerate((0, ROWS - 2)):
        pair = jnp.concatenate([row_of(noise_ref, row), row_of(noise_ref, row + 1)], axis=0)
        aux_ref[2 * at * FL : 2 * (at + 1) * FL, :] = pair.astype(BF16)
    live = iota((1, COLS), 1) < count_ref[...]
    cell = (row_ref[...] * FL + step_ref[...] * 2).astype(F32)
    cell = jnp.where(live, cell, NO_CELL)
    val = val_ref[...]
    high = val.astype(BF16).astype(F32)
    middle = (val - high).astype(BF16).astype(F32)
    low = val - high - middle
    which = iota((16, COLS), 0)
    table = jnp.zeros((16, COLS), F32)
    for at, line in enumerate((cell, col_ref[...].astype(F32), high, middle, low)):
        table = jnp.where(which == at, line, table)
    aux_ref[AUX_OBS:AUX_ROWS, :] = table.astype(BF16)


def weights_kernel(conv_in_ref, conv_out_ref, embed_ref, w1_ref, w2_ref, wide_ref):
    halves = [jnp.zeros((HID, 128), F32), jnp.zeros((HID, 128), F32)]
    wide_ref[...] = jnp.zeros((HID, 128), F32)
    for at in range(9):
        wide_ref[:, 0:18] = conv_in_ref[at].astype(F32)
        start = BLOCK * (at // 3) + GROUP * (at % 3)
        shifted = wide_ref[...]
        if start % 128:
            shifted = pltpu.roll(shifted, start % 128, 1)
        halves[start // 128] = halves[start // 128] + shifted
    square = iota((HID, 128), 0) == iota((HID, 128), 1)
    line = jnp.concatenate([embed_ref[...], jnp.zeros((1, 128 - HID), F32)], axis=1)
    embed = jnp.sum(jnp.where(square, line, 0.0), axis=1, keepdims=True)
    high = embed.astype(BF16).astype(F32)
    middle = (embed - high).astype(BF16).astype(F32)
    low = embed - high - middle
    lane = iota((HID, 128), 1)
    bias = jnp.where(lane == 3 * GROUP, high, 0.0)
    bias = jnp.where(lane == 3 * GROUP + 1, middle, bias)
    bias = jnp.where(lane == 3 * GROUP + 2, low, bias)
    for frame in range(FRAMES):
        left, right = halves
        if frame:
            left = pltpu.roll(left, 2 * frame, 1)
            right = pltpu.roll(right, 2 * frame, 1)
        rows = slice(frame * HID, (frame + 1) * HID)
        w1_ref[rows, 0:128] = (0.5 * (left + bias)).astype(BF16)
        w1_ref[rows, 128:256] = (0.5 * right).astype(BF16)
    odd = iota((FL, HID), 0) % 2 == 1
    parts = []
    for at in range(9):
        upper = conv_out_ref[at, 0:1, :].astype(F32)
        lower = conv_out_ref[at, 1:2, :].astype(F32)
        parts.append(jnp.where(odd, lower, upper))
    stacked = jnp.concatenate(parts, axis=0).astype(BF16)
    shape = (HID, FRAMES * HID)
    spread = jnp.where(iota(shape, 1) % HID == iota(shape, 0), 1.0, 0.0).astype(BF16)
    tiled = jnp.dot(stacked, spread, preferred_element_type=F32)
    mine = (iota(tiled.shape, 0) % FL) // 2 == iota(tiled.shape, 1) // HID
    w2_ref[...] = jnp.where(mine, tiled, 0.0).astype(BF16)


def one_hot_maps(table, first_cell, cells):
    shape = (cells, COLS)
    hit = (iota(shape, 0) + first_cell).astype(F32) == table[0:1, :]
    lines = [jnp.where(hit, 1.0, 0.0)]
    for at in (2, 3, 4):
        lines.append(jnp.where(hit, table[at : at + 1, :], 0.0))
    lhs = jnp.concatenate(lines, axis=0).astype(BF16)
    cols_hot = jnp.where(iota((COLS, COLS), 0).astype(F32) == table[1:2, :], 1.0, 0.0)
    out = lax.dot_general(
        lhs, cols_hot.astype(BF16), (((1,), (1,)), ((), ())), preferred_element_type=F32
    )
    count = out[0:cells]
    total = out[cells : 2 * cells] + out[2 * cells : 3 * cells] + out[3 * cells : 4 * cells]
    return count, total


def maps_kernel(msg_ref, up_ref, down_ref, count_ref, total_ref):
    obs = slice(AUX_OBS, AUX_ROWS)
    pieces = (
        (up_ref, (ROWS - 2) * FL, 2 * FL, 0),
        (msg_ref, 0, ROWS * FL, 2 * FL),
        (down_ref, 0, 2 * FL, (ROWS + 2) * FL),
    )
    for ref, first_cell, cells, at in pieces:
        count, total = one_hot_maps(ref[obs, :].astype(F32), first_cell, cells)
        count_ref[at : at + cells, :] = count
        total_ref[at : at + cells, :] = total


def fill_pair(flags, refs, win_ref, pair, level):
    even, has_prev, has_next = flags
    at = slice(2 * pair * FL, 2 * (pair + 1) * FL)
    core, own, far = (ref[at, :].astype(F32) for ref in refs)
    prev = jnp.where(has_prev, jnp.where(even, far, core), 0.0)
    nxt = jnp.where(has_next, jnp.where(even, core, far), 0.0)
    const = jnp.full((FL, COLS), level, F32)
    for sub in range(2):
        part = slice(sub * FL, (sub + 1) * FL)
        here = jnp.concatenate([prev[part], own[part], nxt[part]], axis=0)
        block = jnp.concatenate(
            [pltpu.roll(here, 1, 1), here, pltpu.roll(here, COLS - 1, 1), const], axis=0
        )
        start = (2 * pair + sub) * BLOCK
        win_ref[start : start + BLOCK, :] = block.astype(BF16)


def run_rows(flags_ref, refs, w1_ref, w2_ref, win_ref, hid_ref, prod_ref, rows, level, emit):
    flags = [flags_ref[at] == 1 for at in range(3)]
    hidden_rows = rows - 2
    n = FRAMES * HID
    win_ref[rows * BLOCK : rows * BLOCK + 16, :] = jnp.zeros((16, COLS), BF16)
    filled = 0
    for step in range(hidden_rows + LAG2 + LAG3):
        want = min(rows, step + 3 + AHEAD)
        while 2 * filled < want:
            fill_pair(flags, refs, win_ref, filled, level)
            filled += 1
        if step < hidden_rows:
            start = step * BLOCK
            half = jnp.dot(w1_ref[...], win_ref[start : start + DEPTH, :], preferred_element_type=F32)
            hid_ref[step * n : (step + 1) * n, :] = (half + half * jnp.tanh(half)).astype(BF16)
        row = step - LAG2
        if 0 <= row < hidden_rows:
            prod_ref[row * 72 : (row + 1) * 72, :] = jnp.dot(
                w2_ref[...], hid_ref[row * n : (row + 1) * n, :], preferred_element_type=F32
            )
        row = step - LAG2 - LAG3
        if row >= 2:
            emit(row - 2)


def net_row(prod_ref, row):
    sums = []
    for col_off in range(3):
        acc = None
        for row_off in range(3):
            at = (row + row_off) * 72 + (3 * row_off + col_off) * FL
            term = prod_ref[at : at + FL, :]
            acc = term if acc is None else acc + term
        sums.append(acc)
    return pltpu.roll(sums[0], 1, 1) + sums[1] + pltpu.roll(sums[2], COLS - 1, 1)


def advance(x, noise, net, count, total, index):
    level, after = LEVELS[index], LEVELS[index + 1]
    spread = level**2 - after**2
    denoised = x * (1.0 / (1.0 + level**2)) + (level / (1.0 + level**2) ** 0.5) * net
    guide = (total - count * denoised) * (1.0 / (OBS_NOISE + COVARIANCE_GAIN * level**2))
    score = (denoised - x) * (1.0 / level**2) + guide
    return x + spread * score + spread**0.5 * noise


def first_kernel(
    flags_ref, x_in, noise_in, aux_up_ref, aux_down_ref, core_ref, own_ref, far_ref, w1_ref,
    w2_ref, count_ref, total_ref, next_ref, send_ref, win_ref, hid_ref, prod_ref, x_ref, noise_ref,
):
    split_halves(x_in, x_ref)
    split_halves(noise_in, noise_ref)
    grow = (1.0 + LEVELS[0] ** 2) ** 0.5
    shrink = 1.0 / (1.0 + LEVELS[1] ** 2) ** 0.5
    made = {}

    def emit(here):
        part = slice((here % 2) * FL, (here % 2 + 1) * FL)
        if not 2 <= here < ROWS + 2:
            at = (here + 2) // 2 * 2 * FL
            x = own_ref[at : at + 2 * FL, :].astype(F32)[part] * grow
            ref, start = (aux_up_ref, 2 * FL) if here < 2 else (aux_down_ref, 0)
            noise = ref[start : start + 2 * FL, :].astype(F32)[part]
        else:
            x, noise = row_of(x_ref, here - 2), row_of(noise_ref, here - 2)
        at = slice(here * FL, (here + 1) * FL)
        new = advance(x, noise, net_row(prod_ref, here), count_ref[at, :], total_ref[at, :], 0)
        if 2 <= here < ROWS + 2:
            next_ref[(here - 2) * FL : (here - 1) * FL, :] = new
        made[here % 2] = new
        if here % 2:
            pair = jnp.concatenate([made[0], made[1]], axis=0) * shrink
            send_ref[(here - 1) * FL : (here + 1) * FL, :] = pair.astype(BF16)

    run_rows(
        flags_ref, (core_ref, own_ref, far_ref), w1_ref, w2_ref, win_ref, hid_ref, prod_ref,
        2 * ROWS, LEVELS[0], emit,
    )


def second_kernel(
    flags_ref, x_ref, noise_in, core_ref, own_ref, far_ref, w1_ref, w2_ref,
    count_ref, total_ref, out_ref, win_ref, hid_ref, prod_ref, noise_ref, half_ref,
):
    split_halves(noise_in, noise_ref)

    def emit(row):
        at = slice((row + 2) * FL, (row + 3) * FL)
        new = advance(
            x_ref[row * FL : (row + 1) * FL, :], row_of(noise_ref, row), net_row(prod_ref, row),
            count_ref[at, :], total_ref[at, :], 1,
        )
        half_ref[pl.ds(row, FL, stride=ROWS), :] = new[:, 0:128]
        half_ref[pl.ds(ROWS * FL + row, FL, stride=ROWS), :] = new[:, 128:256]

    run_rows(
        flags_ref, (core_ref, own_ref, far_ref), w1_ref, w2_ref, win_ref, hid_ref, prod_ref,
        ROWS + 4, LEVELS[1], emit,
    )
    out_ref[:, 0:128] = half_ref[0 : ROWS * FL, :]
    out_ref[:, 128:256] = half_ref[ROWS * FL :, :]


def call(kernel, args, specs, outs, scratch=(), flops=0):
    moved = sum(a.size * a.dtype.itemsize for a in args)
    moved += sum(o.size * o.dtype.itemsize for o in outs)
    return pl.pallas_call(
        kernel,
        out_shape=tuple(outs),
        in_specs=specs,
        out_specs=tuple([VMEM] * len(outs)),
        scratch_shapes=list(scratch),
        compiler_params=params(),
        cost_estimate=pl.CostEstimate(flops=flops, bytes_accessed=moved, transcendentals=0),
    )(*args)


def time_pairs(n_tm, n_rows):
    core, far = [], []
    at = lambda i, r: i * n_rows + r
    for r in range(n_rows):
        for i in range(0, n_tm, 2):
            core += [(at(i, r), at(i + 1, r)), (at(i + 1, r), at(i, r))]
        for i in range(1, n_tm - 1, 2):
            far += [(at(i, r), at(i + 1, r)), (at(i + 1, r), at(i, r))]
        for i in (0, n_tm - 1):
            far.append((at(i, r), at(i, r ^ 1)))
    return core, far


def exchange_rows(block, n_rows):
    up = lax.ppermute(block, "rows", [(i, (i + 1) % n_rows) for i in range(n_rows)])
    if n_rows == 2:
        return up, up
    return up, lax.ppermute(block, "rows", [((i + 1) % n_rows, i) for i in range(n_rows)])


def exchange_time(block, n_tm, n_rows):
    core_pairs, far_pairs = time_pairs(n_tm, n_rows)
    far = lax.ppermute(block, ("tm", "rows"), far_pairs)
    core = lax.ppermute(block, ("tm", "rows"), core_pairs)
    return core, far


def scratch_for(rows):
    halves = pltpu.VMEM((2 * ROWS * FL, 128), F32)
    return [
        pltpu.VMEM((rows * BLOCK + 16, COLS), BF16),
        pltpu.VMEM(((rows - 2) * FRAMES * HID, COLS), BF16),
        pltpu.VMEM(((rows - 2) * 72, COLS), F32),
        halves,
        halves,
    ]


def first_call(*args):
    shape = jax.ShapeDtypeStruct
    return call(
        first_kernel,
        args,
        [SMEM] + [VMEM] * 11,
        [shape((ROWS * FL, COLS), F32), shape(((ROWS + 4) * FL, COLS), BF16)],
        scratch_for(2 * ROWS),
        flops=14 * 2 * 256 * 384 * (256 + 72),
    )


def second_call(*args):
    (out,) = call(
        second_kernel,
        args,
        [SMEM] + [VMEM] * 9,
        [jax.ShapeDtypeStruct((FL * ROWS, COLS), F32)],
        scratch_for(ROWS + 4),
        flops=10 * 2 * 256 * 384 * (256 + 72),
    )
    return out


def per_device(
    noisy_states, noise_first, noise_second, conv_in, conv_out, level_embed,
    obs_count, obs_step, obs_row, obs_col, obs_value,
):
    n_tm, n_rows = lax.axis_size("tm"), lax.axis_size("rows")
    frames, layers, rows, cols = noisy_states.shape
    assert frames == FRAMES and frames * layers == FL and rows == ROWS and cols == COLS
    assert n_tm % 2 == 0 and n_rows % 2 == 0 and obs_step.shape[-1] == COLS
    flat = lambda a: a.reshape(FL * ROWS, COLS)
    line = lambda a: a.reshape(1, -1)
    x, noise_a, noise_b = flat(noisy_states), flat(noise_first), flat(noise_second)
    shape = jax.ShapeDtypeStruct
    here = lax.axis_index("tm")
    flags = jnp.stack(
        [
            (here % 2 == 0).astype(jnp.int32),
            (here > 0).astype(jnp.int32),
            (here < n_tm - 1).astype(jnp.int32),
        ]
    )

    scaled = (x / (1.0 + LEVELS[0] ** 2) ** 0.5).astype(BF16)
    halves = pltpu.VMEM((2 * ROWS * FL, 128), F32)
    (msg,) = call(pack_kernel, (scaled,), [VMEM], [shape((ROWS * FL, COLS), BF16)], [halves])
    (aux,) = call(
        aux_kernel,
        (obs_count, noise_a, line(obs_step), line(obs_row), line(obs_col), line(obs_value)),
        [VMEM] * 6,
        [shape((AUX_ROWS, COLS), BF16)],
        [halves],
    )
    up, down = exchange_rows(msg, n_rows)
    aux_up, aux_down = exchange_rows(aux, n_rows)
    w1, w2 = call(
        weights_kernel,
        (conv_in, conv_out, line(level_embed)),
        [VMEM] * 3,
        [shape((FRAMES * HID, DEPTH), BF16), shape((72, FRAMES * HID), BF16)],
        [pltpu.VMEM((HID, 128), F32)],
    )
    half = ROWS * FL // 2
    own = jnp.concatenate([up[half:], msg, down[:half]], axis=0)
    core, far = exchange_time(own, n_tm, n_rows)
    maps = shape(((ROWS + 4) * FL, COLS), F32)
    count, total = call(maps_kernel, (aux, aux_up, aux_down), [VMEM] * 3, [maps, maps])
    current, send = first_call(
        flags, x, noise_a, aux_up, aux_down, core, own, far, w1, w2, count, total
    )
    core, far = exchange_time(send, n_tm, n_rows)
    out = second_call(flags, current, noise_b, core, send, far, w1, w2, count, total)
    return out.reshape(noisy_states.shape)


def solution(mesh):
    states = P("tm", None, "rows", None)
    slots = P("tm", "rows", None)
    in_specs = (states, states, states, P(), P(), P(), P("tm", "rows"), slots, slots, slots, slots)
    return jax.shard_map(
        per_device, mesh=mesh, in_specs=in_specs, out_specs=states, check_vma=False
    )
```

```python
import jax
import jax.numpy as jnp
from jax import lax
from jax.experimental import pallas as pl
from jax.experimental.pallas import tpu as pltpu
from jax.sharding import PartitionSpec as P


LEVELS = (1.0, 0.5, 0.2)
OBS_NOISE = 0.1
COVARIANCE_GAIN = 0.5

FL = 8
ROWS = 8
COLS = 256
HID = 96
FRAMES = 4
NEAR = 48
FAR = 32
TAPS = 18
TAP_ROWS = 24
DEPTH = 3 * (NEAR + FAR)
AUX_OBS = 4 * FL
AUX_ROWS = AUX_OBS + 16
NO_CELL = 64
AHEAD, LAG2, LAG3 = 4, 3, 3
VMEM = pl.BlockSpec(memory_space=pltpu.VMEM)
SMEM = pl.BlockSpec(memory_space=pltpu.SMEM)
F32 = jnp.float32
BF16 = jnp.bfloat16


def params():
    return pltpu.CompilerParams(vmem_limit_bytes=16 * 1024 * 1024)


def iota(shape, dim):
    return lax.broadcasted_iota(jnp.int32, shape, dim)


def split_halves(ref, halves_ref):
    halves_ref[0 : ROWS * FL, :] = ref[:, 0:128].astype(F32)
    halves_ref[ROWS * FL :, :] = ref[:, 128:256].astype(F32)


def row_of(halves_ref, row):
    left = halves_ref[pl.ds(row, FL, stride=ROWS), :]
    right = halves_ref[pl.ds(ROWS * FL + row, FL, stride=ROWS), :]
    return jnp.concatenate([left, right], axis=1)


def pack_kernel(scaled_in, msg_ref, scaled_ref):
    split_halves(scaled_in, scaled_ref)
    for row in range(0, ROWS, 2):
        pair = jnp.concatenate([row_of(scaled_ref, row), row_of(scaled_ref, row + 1)], axis=0)
        msg_ref[row * FL : (row + 2) * FL, :] = pair.astype(BF16)


def aux_kernel(
    count_ref, noise_in, step_ref, row_ref, col_ref, val_ref, aux_ref, noise_ref
):
    split_halves(noise_in, noise_ref)
    for at, row in enumerate((0, ROWS - 2)):
        pair = jnp.concatenate([row_of(noise_ref, row), row_of(noise_ref, row + 1)], axis=0)
        aux_ref[2 * at * FL : 2 * (at + 1) * FL, :] = pair.astype(BF16)
    live = iota((1, COLS), 1) < count_ref[...]
    cell = jnp.where(live, row_ref[...] * FL + step_ref[...] * 2, NO_CELL).astype(F32)
    val = val_ref[...]
    high = val.astype(BF16).astype(F32)
    middle = (val - high).astype(BF16).astype(F32)
    low = val - high - middle
    which = iota((16, COLS), 0)
    table = jnp.zeros((16, COLS), F32)
    for at, line in enumerate((cell, col_ref[...].astype(F32), high, middle, low)):
        table = jnp.where(which == at, line, table)
    aux_ref[AUX_OBS:AUX_ROWS, :] = table.astype(BF16)


def weights_kernel(flags_ref, taps_ref, conv_out_ref, embed_ref, w1_ref, w2_ref, wide_ref):
    even, has_far = flags_ref[0] == 1, flags_ref[1] == 1
    wide_ref[...] = jnp.zeros((9 * TAP_ROWS, HID), F32)
    for at in range(9):
        wide_ref[at * TAP_ROWS : at * TAP_ROWS + TAPS, :] = taps_ref[at].astype(F32)
    taps = wide_ref[...].astype(BF16)
    square = iota((HID, 128), 0) == iota((HID, 128), 1)
    line = jnp.concatenate([embed_ref[...], jnp.zeros((1, 128 - HID), F32)], axis=1)
    embed = jnp.sum(jnp.where(square, line, 0.0), axis=1, keepdims=True)
    high = embed.astype(BF16).astype(F32)
    middle = (embed - high).astype(BF16).astype(F32)
    low = embed - high - middle
    lane = iota((HID, DEPTH), 1) - (3 * NEAR + 3 * FL)
    bias = jnp.where(lane == 0, high, 0.0)
    bias = jnp.where(lane == 1, middle, bias)
    bias = jnp.where(lane == 2, low, bias)
    shape = (TAP_ROWS, DEPTH)
    lanes = iota(shape, 1)
    for frame in range(FRAMES):
        place = iota(shape, 0) + 2 * frame
        group = place >> 3
        slot = jnp.where(even, 2 - group, group)
        within = place & 7
        parts = []
        for at in range(9):
            row_off, col_off = at // 3, at % 3
            near = row_off * NEAR + col_off * 2 * FL + slot * FL + within
            far = 3 * NEAR + row_off * FAR + col_off * FL + within
            target = jnp.where(slot == 2, jnp.where(has_far, far, -1), near)
            parts.append(jnp.where(lanes == target, 0.5, 0.0))
        move = jnp.concatenate(parts, axis=0).astype(BF16)
        out = lax.dot_general(
            taps, move, (((0,), (0,)), ((), ())), preferred_element_type=F32
        )
        w1_ref[frame * HID : (frame + 1) * HID, :] = (out + 0.5 * bias).astype(BF16)
    odd = iota((FL, HID), 0) % 2 == 1
    parts = []
    for at in range(9):
        upper = conv_out_ref[at, 0:1, :].astype(F32)
        lower = conv_out_ref[at, 1:2, :].astype(F32)
        parts.append(jnp.where(odd, lower, upper))
    stacked = jnp.concatenate(parts, axis=0).astype(BF16)
    shape = (HID, FRAMES * HID)
    spread = jnp.where(iota(shape, 1) % HID == iota(shape, 0), 1.0, 0.0).astype(BF16)
    tiled = jnp.dot(stacked, spread, preferred_element_type=F32)
    mine = (iota(tiled.shape, 0) % FL) // 2 == iota(tiled.shape, 1) // HID
    w2_ref[...] = jnp.where(mine, tiled, 0.0).astype(BF16)


def one_hot_maps(table, first_cell, cells):
    shape = (cells, COLS)
    hit = (iota(shape, 0) + first_cell).astype(F32) == table[0:1, :]
    lines = [jnp.where(hit, 1.0, 0.0)]
    for at in (2, 3, 4):
        lines.append(jnp.where(hit, table[at : at + 1, :], 0.0))
    lhs = jnp.concatenate(lines, axis=0).astype(BF16)
    cols_hot = jnp.where(iota((COLS, COLS), 0).astype(F32) == table[1:2, :], 1.0, 0.0)
    out = lax.dot_general(
        lhs, cols_hot.astype(BF16), (((1,), (1,)), ((), ())), preferred_element_type=F32
    )
    count = out[0:cells]
    total = out[cells : 2 * cells] + out[2 * cells : 3 * cells] + out[3 * cells : 4 * cells]
    return count, total


def maps_kernel(msg_ref, up_ref, down_ref, count_ref, total_ref):
    obs = slice(AUX_OBS, AUX_ROWS)
    pieces = (
        (up_ref, (ROWS - 2) * FL, 2 * FL, 0),
        (msg_ref, 0, ROWS * FL, 2 * FL),
        (down_ref, 0, 2 * FL, (ROWS + 2) * FL),
    )
    for ref, first_cell, cells, at in pieces:
        count, total = one_hot_maps(ref[obs, :].astype(F32), first_cell, cells)
        count_ref[at : at + cells, :] = count
        total_ref[at : at + cells, :] = total


def shifts(here):
    return [pltpu.roll(here, 1, 1), here, pltpu.roll(here, COLS - 1, 1)]


def near_kernel(core_ref, own_ref, near_ref):
    for pair in range(own_ref.shape[0] // (2 * FL)):
        at = slice(2 * pair * FL, 2 * (pair + 1) * FL)
        core, own = core_ref[at, :].astype(F32), own_ref[at, :].astype(F32)
        for sub in range(2):
            part = slice(sub * FL, (sub + 1) * FL)
            here = jnp.concatenate([core[part], own[part]], axis=0)
            block = jnp.concatenate(shifts(here), axis=0)
            start = (2 * pair + sub) * NEAR
            near_ref[start : start + NEAR, :] = block.astype(BF16)


def fill_pair(ref, win_ref, pair, level):
    far = ref[2 * pair * FL : 2 * (pair + 1) * FL, :].astype(F32)
    const = jnp.full((FL, COLS), level, F32)
    for sub in range(2):
        here = far[sub * FL : (sub + 1) * FL]
        block = jnp.concatenate(shifts(here) + [const], axis=0)
        start = (2 * pair + sub) * FAR
        win_ref[start : start + FAR, :] = block.astype(BF16)


def run_rows(near_ref, far_ref, w1_ref, w2_ref, win_ref, hid_ref, prod_ref, rows, level, emit):
    hidden_rows = rows - 2
    n = FRAMES * HID
    filled = 0
    for step in range(hidden_rows + LAG2 + LAG3):
        want = min(rows, step + 3 + AHEAD)
        while 2 * filled < want:
            fill_pair(far_ref, win_ref, filled, level)
            filled += 1
        if step < hidden_rows:
            near = near_ref[step * NEAR : (step + 3) * NEAR, :]
            far = win_ref[step * FAR : (step + 3) * FAR, :]
            window = jnp.concatenate([near, far], axis=0)
            half = jnp.dot(w1_ref[...], window, preferred_element_type=F32)
            hid_ref[step * n : (step + 1) * n, :] = (half + half * jnp.tanh(half)).astype(BF16)
        row = step - LAG2
        if 0 <= row < hidden_rows:
            prod_ref[row * 72 : (row + 1) * 72, :] = jnp.dot(
                w2_ref[...], hid_ref[row * n : (row + 1) * n, :], preferred_element_type=F32
            )
        row = step - LAG2 - LAG3
        if row >= 2:
            emit(row - 2)


def net_row(prod_ref, row):
    sums = []
    for col_off in range(3):
        acc = None
        for row_off in range(3):
            at = (row + row_off) * 72 + (3 * row_off + col_off) * FL
            term = prod_ref[at : at + FL, :]
            acc = term if acc is None else acc + term
        sums.append(acc)
    return pltpu.roll(sums[0], 1, 1) + sums[1] + pltpu.roll(sums[2], COLS - 1, 1)


def advance(x, noise, net, count, total, index):
    level, after = LEVELS[index], LEVELS[index + 1]
    spread = level**2 - after**2
    denoised = x * (1.0 / (1.0 + level**2)) + (level / (1.0 + level**2) ** 0.5) * net
    guide = (total - count * denoised) * (1.0 / (OBS_NOISE + COVARIANCE_GAIN * level**2))
    score = (denoised - x) * (1.0 / level**2) + guide
    return x + spread * score + spread**0.5 * noise


def first_kernel(
    x_in, noise_in, aux_up_ref, aux_down_ref, near_ref, own_ref, far_ref, w1_ref, w2_ref,
    count_ref, total_ref, next_ref, send_ref, win_ref, hid_ref, prod_ref, x_ref, noise_ref,
):
    split_halves(x_in, x_ref)
    split_halves(noise_in, noise_ref)
    grow = (1.0 + LEVELS[0] ** 2) ** 0.5
    shrink = 1.0 / (1.0 + LEVELS[1] ** 2) ** 0.5
    made = {}

    def emit(here):
        part = slice((here % 2) * FL, (here % 2 + 1) * FL)
        if not 2 <= here < ROWS + 2:
            at = (here + 2) // 2 * 2 * FL
            x = own_ref[at : at + 2 * FL, :].astype(F32)[part] * grow
            ref, start = (aux_up_ref, 2 * FL) if here < 2 else (aux_down_ref, 0)
            noise = ref[start : start + 2 * FL, :].astype(F32)[part]
        else:
            x, noise = row_of(x_ref, here - 2), row_of(noise_ref, here - 2)
        at = slice(here * FL, (here + 1) * FL)
        new = advance(x, noise, net_row(prod_ref, here), count_ref[at, :], total_ref[at, :], 0)
        if 2 <= here < ROWS + 2:
            next_ref[(here - 2) * FL : (here - 1) * FL, :] = new
        made[here % 2] = new
        if here % 2:
            pair = jnp.concatenate([made[0], made[1]], axis=0) * shrink
            send_ref[(here - 1) * FL : (here + 1) * FL, :] = pair.astype(BF16)

    run_rows(
        near_ref, far_ref, w1_ref, w2_ref, win_ref, hid_ref, prod_ref, 2 * ROWS, LEVELS[0], emit
    )


def second_kernel(
    x_ref, noise_in, near_ref, far_ref, w1_ref, w2_ref,
    count_ref, total_ref, out_ref, win_ref, hid_ref, prod_ref, noise_ref, half_ref,
):
    split_halves(noise_in, noise_ref)

    def emit(row):
        at = slice((row + 2) * FL, (row + 3) * FL)
        new = advance(
            x_ref[row * FL : (row + 1) * FL, :], row_of(noise_ref, row), net_row(prod_ref, row),
            count_ref[at, :], total_ref[at, :], 1,
        )
        half_ref[pl.ds(row, FL, stride=ROWS), :] = new[:, 0:128]
        half_ref[pl.ds(ROWS * FL + row, FL, stride=ROWS), :] = new[:, 128:256]

    run_rows(
        near_ref, far_ref, w1_ref, w2_ref, win_ref, hid_ref, prod_ref, ROWS + 4, LEVELS[1], emit
    )
    out_ref[:, 0:128] = half_ref[0 : ROWS * FL, :]
    out_ref[:, 128:256] = half_ref[ROWS * FL :, :]


def call(kernel, args, specs, outs, scratch=(), flops=0):
    moved = sum(a.size * a.dtype.itemsize for a in args)
    moved += sum(o.size * o.dtype.itemsize for o in outs)
    return pl.pallas_call(
        kernel,
        out_shape=tuple(outs),
        in_specs=specs,
        out_specs=tuple([VMEM] * len(outs)),
        scratch_shapes=list(scratch),
        compiler_params=params(),
        cost_estimate=pl.CostEstimate(flops=flops, bytes_accessed=moved, transcendentals=0),
    )(*args)


def time_pairs(n_tm, n_rows):
    core, far = [], []
    at = lambda i, r: i * n_rows + r
    for r in range(n_rows):
        for i in range(0, n_tm, 2):
            core += [(at(i, r), at(i + 1, r)), (at(i + 1, r), at(i, r))]
        for i in range(1, n_tm - 1, 2):
            far += [(at(i, r), at(i + 1, r)), (at(i + 1, r), at(i, r))]
        for i in (0, n_tm - 1):
            far.append((at(i, r), at(i, r ^ 1)))
    return core, far


def exchange_rows(block, n_rows):
    up = lax.ppermute(block, "rows", [(i, (i + 1) % n_rows) for i in range(n_rows)])
    if n_rows == 2:
        return up, up
    return up, lax.ppermute(block, "rows", [((i + 1) % n_rows, i) for i in range(n_rows)])


def exchange_time(block, n_tm, n_rows):
    core_pairs, far_pairs = time_pairs(n_tm, n_rows)
    far = lax.ppermute(block, ("tm", "rows"), far_pairs)
    core = lax.ppermute(block, ("tm", "rows"), core_pairs)
    return core, far


def scratch_for(rows):
    halves = pltpu.VMEM((2 * ROWS * FL, 128), F32)
    return [
        pltpu.VMEM((rows * FAR, COLS), BF16),
        pltpu.VMEM(((rows - 2) * FRAMES * HID, COLS), BF16),
        pltpu.VMEM(((rows - 2) * 72, COLS), F32),
        halves,
        halves,
    ]


def near_call(core, own):
    rows = own.shape[0] // FL
    (near,) = call(
        near_kernel, (core, own), [VMEM] * 2, [jax.ShapeDtypeStruct((rows * NEAR, COLS), BF16)]
    )
    return near


def first_call(*args):
    shape = jax.ShapeDtypeStruct
    return call(
        first_kernel,
        args,
        [VMEM] * 11,
        [shape((ROWS * FL, COLS), F32), shape(((ROWS + 4) * FL, COLS), BF16)],
        scratch_for(2 * ROWS),
        flops=14 * 2 * 256 * 384 * (256 + 72),
    )


def second_call(*args):
    (out,) = call(
        second_kernel,
        args,
        [VMEM] * 8,
        [jax.ShapeDtypeStruct((FL * ROWS, COLS), F32)],
        scratch_for(ROWS + 4),
        flops=10 * 2 * 256 * 384 * (256 + 72),
    )
    return out


def per_device(
    noisy_states, noise_first, noise_second, conv_in, conv_out, level_embed,
    obs_count, obs_step, obs_row, obs_col, obs_value,
):
    n_tm, n_rows = lax.axis_size("tm"), lax.axis_size("rows")
    frames, layers, rows, cols = noisy_states.shape
    assert frames == FRAMES and frames * layers == FL and rows == ROWS and cols == COLS
    assert n_tm % 2 == 0 and n_rows % 2 == 0 and obs_step.shape[-1] == COLS
    flat = lambda a: a.reshape(FL * ROWS, COLS)
    line = lambda a: a.reshape(1, -1)
    x, noise_a, noise_b = flat(noisy_states), flat(noise_first), flat(noise_second)
    shape = jax.ShapeDtypeStruct
    here = lax.axis_index("tm")
    even = here % 2 == 0
    has_far = jnp.where(even, here > 0, here < n_tm - 1)
    flags = jnp.stack([even, has_far]).astype(jnp.int32)
    scaled = (x / (1.0 + LEVELS[0] ** 2) ** 0.5).astype(BF16)
    halves = pltpu.VMEM((2 * ROWS * FL, 128), F32)
    (msg,) = call(pack_kernel, (scaled,), [VMEM], [shape((ROWS * FL, COLS), BF16)], [halves])
    (aux,) = call(
        aux_kernel,
        (obs_count, noise_a, line(obs_step), line(obs_row), line(obs_col), line(obs_value)),
        [VMEM] * 6,
        [shape((AUX_ROWS, COLS), BF16)],
        [halves],
    )
    up, down = exchange_rows(msg, n_rows)
    aux_up, aux_down = exchange_rows(aux, n_rows)
    w1, w2 = call(
        weights_kernel,
        (flags, conv_in.transpose(0, 2, 1), conv_out, line(level_embed)),
        [SMEM] + [VMEM] * 3,
        [shape((FRAMES * HID, DEPTH), BF16), shape((72, FRAMES * HID), BF16)],
        [pltpu.VMEM((9 * TAP_ROWS, HID), F32)],
    )
    half = ROWS * FL // 2
    own = jnp.concatenate([up[half:], msg, down[:half]], axis=0)
    core, far = exchange_time(own, n_tm, n_rows)
    maps = shape(((ROWS + 4) * FL, COLS), F32)
    count, total = call(maps_kernel, (aux, aux_up, aux_down), [VMEM] * 3, [maps, maps])
    near = near_call(core, own)
    current, send = first_call(
        x, noise_a, aux_up, aux_down, near, own, far, w1, w2, count, total
    )
    core, far = exchange_time(send, n_tm, n_rows)
    near = near_call(core, send)
    out = second_call(current, noise_b, near, far, w1, w2, count, total)
    return out.reshape(noisy_states.shape)


def solution(mesh):
    states = P("tm", None, "rows", None)
    slots = P("tm", "rows", None)
    in_specs = (states, states, states, P(), P(), P(), P("tm", "rows"), slots, slots, slots, slots)
    return jax.shard_map(
        per_device, mesh=mesh, in_specs=in_specs, out_specs=states, check_vma=False
    )
```

```python
import functools

import jax
import jax.numpy as jnp
from jax import lax
from jax.experimental import pallas as pl
from jax.experimental.pallas import tpu as pltpu
from jax.sharding import PartitionSpec as P


LEVELS = (1.0, 0.5, 0.2)
OBS_NOISE = 0.1
COVARIANCE_GAIN = 0.5

FL = 8
ROWS = 8
COLS = 256
HID = 96
FRAMES = 4
NEAR = 48
FAR = 32
TAPS = 18
TAP_ROWS = 24
DEPTH = 3 * (NEAR + FAR)
EDGE = 4 * FL
AUX_OBS = 2 * EDGE
AUX_ROWS = AUX_OBS + 16
NO_CELL = 64
AHEAD, LAG2, LAG3 = 4, 4, 4
GROW = (1.0 + LEVELS[0] ** 2) ** 0.5
VMEM = pl.BlockSpec(memory_space=pltpu.VMEM)
F32 = jnp.float32
BF16 = jnp.bfloat16


def params():
    return pltpu.CompilerParams(vmem_limit_bytes=16 * 1024 * 1024)


def iota(shape, dim):
    return lax.broadcasted_iota(jnp.int32, shape, dim)


def split_halves(ref, halves_ref):
    halves_ref[0 : ROWS * FL, :] = ref[:, 0:128].astype(F32)
    halves_ref[ROWS * FL :, :] = ref[:, 128:256].astype(F32)


def row_of(halves_ref, row):
    left = halves_ref[pl.ds(row, FL, stride=ROWS), :]
    right = halves_ref[pl.ds(ROWS * FL + row, FL, stride=ROWS), :]
    return jnp.concatenate([left, right], axis=1)


def pack_kernel(scaled_in, msg_ref, scaled_ref):
    split_halves(scaled_in, scaled_ref)
    for row in range(0, ROWS, 2):
        pair = jnp.concatenate([row_of(scaled_ref, row), row_of(scaled_ref, row + 1)], axis=0)
        msg_ref[row * FL : (row + 2) * FL, :] = pair.astype(BF16)


def aux_kernel(
    count_ref, msg_ref, x_in, noise_in, step_ref, row_ref, col_ref, val_ref, aux_ref, x_ref,
    noise_ref, x_halves, noise_halves,
):
    split_halves(x_in, x_halves)
    split_halves(noise_in, noise_halves)
    for row in range(ROWS):
        x_ref[row * FL : (row + 1) * FL, :] = row_of(x_halves, row)
        noise_ref[row * FL : (row + 1) * FL, :] = row_of(noise_halves, row)
    for at, row in enumerate((0, ROWS - 2)):
        pair = slice(row * FL, (row + 2) * FL)
        rest = x_ref[pair, :] - msg_ref[pair, :].astype(F32) * GROW
        for part, value in enumerate((noise_ref[pair, :], rest)):
            start = part * EDGE + 2 * at * FL
            aux_ref[start : start + 2 * FL, :] = value.astype(BF16)
    live = iota((1, COLS), 1) < count_ref[...]
    cell = jnp.where(live, row_ref[...] * FL + step_ref[...] * 2, NO_CELL).astype(F32)
    val = val_ref[...]
    high = val.astype(BF16).astype(F32)
    middle = (val - high).astype(BF16).astype(F32)
    low = val - high - middle
    which = iota((16, COLS), 0)
    table = jnp.zeros((16, COLS), F32)
    for at, line in enumerate((cell, col_ref[...].astype(F32), high, middle, low)):
        table = jnp.where(which == at, line, table)
    aux_ref[AUX_OBS:AUX_ROWS, :] = table.astype(BF16)


def weights_kernel(n_tm, taps_ref, conv_out_ref, embed_ref, w1_ref, w2_ref, wide_ref):
    here = lax.axis_index("tm")
    even = lax.rem(here, 2) == 0
    has_far = jnp.logical_and(here > 0, here < n_tm - 1)
    wide_ref[...] = jnp.zeros(wide_ref.shape, F32)
    for at in range(9):
        tap = taps_ref[at].astype(F32)
        for frame in range(FRAMES):
            start = at * TAP_ROWS + 2 * frame
            wide_ref[start : start + TAPS, frame * 128 : frame * 128 + HID] = tap
    square = iota((HID, 128), 0) == iota((HID, 128), 1)
    line = jnp.concatenate([embed_ref[...], jnp.zeros((1, 128 - HID), F32)], axis=1)
    embed = jnp.sum(jnp.where(square, line, 0.0), axis=1, keepdims=True)
    high = embed.astype(BF16).astype(F32)
    middle = (embed - high).astype(BF16).astype(F32)
    low = embed - high - middle
    lane = iota((HID, DEPTH), 1) - (3 * NEAR + 3 * FL)
    bias = jnp.where(lane == 0, high, 0.0)
    bias = jnp.where(lane == 1, middle, bias)
    bias = jnp.where(lane == 2, low, bias)
    shape = (TAP_ROWS, DEPTH)
    lanes = iota(shape, 1)
    group = iota(shape, 0) >> 3
    within = iota(shape, 0) & 7
    slot = jnp.where(even, 2 - group, group)
    near = slot * FL + within
    far = jnp.where(has_far, 3 * NEAR + within, -DEPTH)
    parts = []
    for at in range(9):
        row_off, col_off = at // 3, at % 3
        near_start = row_off * NEAR + col_off * 2 * FL
        far_start = row_off * FAR + col_off * FL
        target = jnp.where(slot == 2, far + far_start, near + near_start)
        parts.append(jnp.where(lanes == target, 0.5, 0.0))
    move = jnp.concatenate(parts, axis=0).astype(BF16)
    for frame in range(FRAMES):
        taps = wide_ref[:, frame * 128 : (frame + 1) * 128].T[0:HID, :].astype(BF16)
        out = jnp.dot(taps, move, preferred_element_type=F32)
        w1_ref[frame * HID : (frame + 1) * HID, :] = (out + 0.5 * bias).astype(BF16)
    odd = iota((FL, HID), 0) % 2 == 1
    parts = []
    for at in range(9):
        upper = conv_out_ref[at, 0:1, :].astype(F32)
        lower = conv_out_ref[at, 1:2, :].astype(F32)
        parts.append(jnp.where(odd, lower, upper))
    stacked = jnp.concatenate(parts, axis=0).astype(BF16)
    shape = (HID, FRAMES * HID)
    spread = jnp.where(iota(shape, 1) % HID == iota(shape, 0), 1.0, 0.0).astype(BF16)
    tiled = jnp.dot(stacked, spread, preferred_element_type=F32)
    mine = (iota(tiled.shape, 0) % FL) // 2 == iota(tiled.shape, 1) // HID
    w2_ref[...] = jnp.where(mine, tiled, 0.0).astype(BF16)


def one_hot_maps(table, first_cell, cells):
    shape = (cells, COLS)
    hit = (iota(shape, 0) + first_cell).astype(F32) == table[0:1, :]
    lines = [jnp.where(hit, 1.0, 0.0)]
    for at in (2, 3, 4):
        lines.append(jnp.where(hit, table[at : at + 1, :], 0.0))
    lhs = jnp.concatenate(lines, axis=0).astype(BF16)
    cols_hot = jnp.where(iota((COLS, COLS), 0).astype(F32) == table[1:2, :], 1.0, 0.0)
    out = lax.dot_general(
        lhs, cols_hot.astype(BF16), (((1,), (1,)), ((), ())), preferred_element_type=F32
    )
    count = out[0:cells]
    total = out[cells : 2 * cells] + out[2 * cells : 3 * cells] + out[3 * cells : 4 * cells]
    return count, total


def maps_kernel(msg_ref, up_ref, down_ref, count_ref, total_ref):
    obs = slice(AUX_OBS, AUX_ROWS)
    pieces = (
        (up_ref, (ROWS - 2) * FL, 2 * FL, 0),
        (msg_ref, 0, ROWS * FL, 2 * FL),
        (down_ref, 0, 2 * FL, (ROWS + 2) * FL),
    )
    for ref, first_cell, cells, at in pieces:
        count, total = one_hot_maps(ref[obs, :].astype(F32), first_cell, cells)
        count_ref[at : at + cells, :] = count
        total_ref[at : at + cells, :] = total


def shifts(here):
    return [pltpu.roll(here, 1, 1), here, pltpu.roll(here, COLS - 1, 1)]


def near_kernel(core_ref, own_ref, near_ref):
    for pair in range(own_ref.shape[0] // (2 * FL)):
        at = slice(2 * pair * FL, 2 * (pair + 1) * FL)
        core, own = core_ref[at, :].astype(F32), own_ref[at, :].astype(F32)
        for sub in range(2):
            part = slice(sub * FL, (sub + 1) * FL)
            here = jnp.concatenate([core[part], own[part]], axis=0)
            block = jnp.concatenate(shifts(here), axis=0)
            start = (2 * pair + sub) * NEAR
            near_ref[start : start + NEAR, :] = block.astype(BF16)


def fill_pair(ref, win_ref, pair, level):
    far = ref[2 * pair * FL : 2 * (pair + 1) * FL, :].astype(F32)
    const = jnp.full((FL, COLS), level, F32)
    for sub in range(2):
        here = far[sub * FL : (sub + 1) * FL]
        block = jnp.concatenate(shifts(here) + [const], axis=0)
        start = (2 * pair + sub) * FAR
        win_ref[start : start + FAR, :] = block.astype(BF16)


def run_rows(near_ref, far_ref, w1_ref, w2_ref, win_ref, hid_ref, prod_ref, rows, level, emit):
    hidden_rows = rows - 2
    n = FRAMES * HID
    filled = 0
    for step in range(hidden_rows + LAG2 + LAG3):
        want = min(rows, step + 3 + AHEAD)
        while 2 * filled < want:
            fill_pair(far_ref, win_ref, filled, level)
            filled += 1
        if step < hidden_rows:
            near = near_ref[step * NEAR : (step + 3) * NEAR, :]
            far = win_ref[step * FAR : (step + 3) * FAR, :]
            window = jnp.concatenate([near, far], axis=0)
            half = jnp.dot(w1_ref[...], window, preferred_element_type=F32)
            hid_ref[step * n : (step + 1) * n, :] = (half + half * jnp.tanh(half)).astype(BF16)
        row = step - LAG2
        if 0 <= row < hidden_rows:
            prod_ref[row * 72 : (row + 1) * 72, :] = jnp.dot(
                w2_ref[...], hid_ref[row * n : (row + 1) * n, :], preferred_element_type=F32
            )
        row = step - LAG2 - LAG3
        if row >= 2:
            emit(row - 2)


def net_row(prod_ref, row):
    sums = []
    for col_off in range(3):
        acc = None
        for row_off in range(3):
            at = (row + row_off) * 72 + (3 * row_off + col_off) * FL
            term = prod_ref[at : at + FL, :]
            acc = term if acc is None else acc + term
        sums.append(acc)
    return pltpu.roll(sums[0], 1, 1) + sums[1] + pltpu.roll(sums[2], COLS - 1, 1)


def advance(x, noise, net, count, total, index):
    level, after = LEVELS[index], LEVELS[index + 1]
    spread = level**2 - after**2
    denoised = x * (1.0 / (1.0 + level**2)) + (level / (1.0 + level**2) ** 0.5) * net
    guide = (total - count * denoised) * (1.0 / (OBS_NOISE + COVARIANCE_GAIN * level**2))
    score = (denoised - x) * (1.0 / level**2) + guide
    return x + spread * score + spread**0.5 * noise


def first_kernel(
    x_ref, noise_ref, aux_up_ref, aux_down_ref, near_ref, own_ref, far_ref, w1_ref, w2_ref,
    count_ref, total_ref, next_ref, send_ref, win_ref, hid_ref, prod_ref,
):
    shrink = 1.0 / (1.0 + LEVELS[1] ** 2) ** 0.5
    made = {}

    def emit(here):
        part = slice((here % 2) * FL, (here % 2 + 1) * FL)
        if not 2 <= here < ROWS + 2:
            at = (here + 2) // 2 * 2 * FL
            ref, start = (aux_up_ref, 2 * FL) if here < 2 else (aux_down_ref, 0)
            noise, rest = (
                ref[start + piece * EDGE : start + piece * EDGE + 2 * FL, :].astype(F32)[part]
                for piece in range(2)
            )
            x = own_ref[at : at + 2 * FL, :].astype(F32)[part] * GROW + rest
        else:
            inner = slice((here - 2) * FL, (here - 1) * FL)
            x, noise = x_ref[inner, :], noise_ref[inner, :]
        at = slice(here * FL, (here + 1) * FL)
        new = advance(x, noise, net_row(prod_ref, here), count_ref[at, :], total_ref[at, :], 0)
        if 2 <= here < ROWS + 2:
            next_ref[(here - 2) * FL : (here - 1) * FL, :] = new
        made[here % 2] = new
        if here % 2:
            pair = jnp.concatenate([made[0], made[1]], axis=0) * shrink
            send_ref[(here - 1) * FL : (here + 1) * FL, :] = pair.astype(BF16)

    run_rows(
        near_ref, far_ref, w1_ref, w2_ref, win_ref, hid_ref, prod_ref, 2 * ROWS, LEVELS[0], emit
    )


def second_kernel(
    x_ref, noise_in, near_ref, far_ref, w1_ref, w2_ref,
    count_ref, total_ref, out_ref, win_ref, hid_ref, prod_ref, noise_ref, half_ref,
):
    split_halves(noise_in, noise_ref)

    def emit(row):
        at = slice((row + 2) * FL, (row + 3) * FL)
        new = advance(
            x_ref[row * FL : (row + 1) * FL, :], row_of(noise_ref, row), net_row(prod_ref, row),
            count_ref[at, :], total_ref[at, :], 1,
        )
        half_ref[pl.ds(row, FL, stride=ROWS), :] = new[:, 0:128]
        half_ref[pl.ds(ROWS * FL + row, FL, stride=ROWS), :] = new[:, 128:256]

    run_rows(
        near_ref, far_ref, w1_ref, w2_ref, win_ref, hid_ref, prod_ref, ROWS + 4, LEVELS[1], emit
    )
    out_ref[:, 0:128] = half_ref[0 : ROWS * FL, :]
    out_ref[:, 128:256] = half_ref[ROWS * FL :, :]


def call(kernel, args, specs, outs, scratch=(), flops=0):
    moved = sum(a.size * a.dtype.itemsize for a in args)
    moved += sum(o.size * o.dtype.itemsize for o in outs)
    return pl.pallas_call(
        kernel,
        out_shape=tuple(outs),
        in_specs=specs,
        out_specs=tuple([VMEM] * len(outs)),
        scratch_shapes=list(scratch),
        compiler_params=params(),
        cost_estimate=pl.CostEstimate(flops=flops, bytes_accessed=moved, transcendentals=0),
    )(*args)


def time_pairs(n_tm, n_rows):
    core, far = [], []
    at = lambda i, r: i * n_rows + r
    for r in range(n_rows):
        for i in range(0, n_tm, 2):
            core += [(at(i, r), at(i + 1, r)), (at(i + 1, r), at(i, r))]
        for i in range(1, n_tm - 1, 2):
            far += [(at(i, r), at(i + 1, r)), (at(i + 1, r), at(i, r))]
        for i in (0, n_tm - 1):
            far.append((at(i, r), at(i, r ^ 1)))
    return core, far


def exchange_rows(block, n_rows):
    up = lax.ppermute(block, "rows", [(i, (i + 1) % n_rows) for i in range(n_rows)])
    if n_rows == 2:
        return up, up
    return up, lax.ppermute(block, "rows", [((i + 1) % n_rows, i) for i in range(n_rows)])


def exchange_time(block, n_tm, n_rows):
    core_pairs, far_pairs = time_pairs(n_tm, n_rows)
    far = lax.ppermute(block, ("tm", "rows"), far_pairs)
    core = lax.ppermute(block, ("tm", "rows"), core_pairs)
    return core, far


def scratch_for(rows):
    halves = pltpu.VMEM((2 * ROWS * FL, 128), F32)
    return [
        pltpu.VMEM((rows * FAR, COLS), BF16),
        pltpu.VMEM(((rows - 2) * FRAMES * HID, COLS), BF16),
        pltpu.VMEM(((rows - 2) * 72, COLS), F32),
        halves,
        halves,
    ]


def near_call(core, own):
    rows = own.shape[0] // FL
    (near,) = call(
        near_kernel, (core, own), [VMEM] * 2, [jax.ShapeDtypeStruct((rows * NEAR, COLS), BF16)]
    )
    return near


def first_call(*args):
    shape = jax.ShapeDtypeStruct
    return call(
        first_kernel,
        args,
        [VMEM] * 11,
        [shape((ROWS * FL, COLS), F32), shape(((ROWS + 4) * FL, COLS), BF16)],
        scratch_for(2 * ROWS)[:3],
        flops=14 * 2 * 256 * 384 * (256 + 72),
    )


def second_call(*args):
    (out,) = call(
        second_kernel,
        args,
        [VMEM] * 8,
        [jax.ShapeDtypeStruct((FL * ROWS, COLS), F32)],
        scratch_for(ROWS + 4),
        flops=10 * 2 * 256 * 384 * (256 + 72),
    )
    return out


def per_device(
    noisy_states, noise_first, noise_second, conv_in, conv_out, level_embed,
    obs_count, obs_step, obs_row, obs_col, obs_value,
):
    n_tm, n_rows = lax.axis_size("tm"), lax.axis_size("rows")
    frames, layers, rows, cols = noisy_states.shape
    assert frames == FRAMES and frames * layers == FL and rows == ROWS and cols == COLS
    assert n_tm % 2 == 0 and n_rows % 2 == 0 and obs_step.shape[-1] == COLS
    flat = lambda a: a.reshape(FL * ROWS, COLS)
    line = lambda a: a.reshape(1, -1)
    x, noise_a, noise_b = flat(noisy_states), flat(noise_first), flat(noise_second)
    shape = jax.ShapeDtypeStruct
    scaled = (x / (1.0 + LEVELS[0] ** 2) ** 0.5).astype(BF16)
    halves = pltpu.VMEM((2 * ROWS * FL, 128), F32)
    (msg,) = call(pack_kernel, (scaled,), [VMEM], [shape((ROWS * FL, COLS), BF16)], [halves])
    grid = shape((ROWS * FL, COLS), F32)
    aux, x_rows, noise_rows = call(
        aux_kernel,
        (obs_count, msg, x, noise_a, line(obs_step), line(obs_row), line(obs_col), line(obs_value)),
        [VMEM] * 8,
        [shape((AUX_ROWS, COLS), BF16), grid, grid],
        [halves, halves],
    )
    up, down = exchange_rows(msg, n_rows)
    aux_up, aux_down = exchange_rows(aux, n_rows)
    w1, w2 = call(
        functools.partial(weights_kernel, n_tm),
        (conv_in.transpose(0, 2, 1), conv_out, line(level_embed)),
        [VMEM] * 3,
        [shape((FRAMES * HID, DEPTH), BF16), shape((72, FRAMES * HID), BF16)],
        [pltpu.VMEM((9 * TAP_ROWS, FRAMES * 128), F32)],
    )
    half = ROWS * FL // 2
    own = jnp.concatenate([up[half:], msg, down[:half]], axis=0)
    core, far = exchange_time(own, n_tm, n_rows)
    maps = shape(((ROWS + 4) * FL, COLS), F32)
    count, total = call(maps_kernel, (aux, aux_up, aux_down), [VMEM] * 3, [maps, maps])
    near = near_call(core, own)
    current, send = first_call(
        x_rows, noise_rows, aux_up, aux_down, near, own, far, w1, w2, count, total
    )
    core, far = exchange_time(send, n_tm, n_rows)
    near = near_call(core, send)
    out = second_call(current, noise_b, near, far, w1, w2, count, total)
    return out.reshape(noisy_states.shape)


def solution(mesh):
    states = P("tm", None, "rows", None)
    slots = P("tm", "rows", None)
    in_specs = (states, states, states, P(), P(), P(), P("tm", "rows"), slots, slots, slots, slots)
    return jax.shard_map(
        per_device, mesh=mesh, in_specs=in_specs, out_specs=states, check_vma=False
    )
```

```python
import functools

import jax
import jax.numpy as jnp
from jax import lax
from jax.experimental import pallas as pl
from jax.experimental.pallas import tpu as pltpu
from jax.sharding import PartitionSpec as P


LEVELS = (1.0, 0.5, 0.2)
OBS_NOISE = 0.1
COVARIANCE_GAIN = 0.5

FL = 8
ROWS = 8
COLS = 256
HID = 96
FRAMES = 4
NEAR = 48
FAR = 32
TAPS = 18
TAP_ROWS = 24
DEPTH = 3 * (NEAR + FAR)
AUX_OBS = 4 * FL
AUX_ROWS = AUX_OBS + 16
NO_CELL = 64
AHEAD, LAG2, LAG3 = 4, 4, 4
VMEM = pl.BlockSpec(memory_space=pltpu.VMEM)
F32 = jnp.float32
BF16 = jnp.bfloat16


def params():
    return pltpu.CompilerParams(vmem_limit_bytes=16 * 1024 * 1024)


def iota(shape, dim):
    return lax.broadcasted_iota(jnp.int32, shape, dim)


def split_halves(ref, halves_ref):
    halves_ref[0 : ROWS * FL, :] = ref[:, 0:128].astype(F32)
    halves_ref[ROWS * FL :, :] = ref[:, 128:256].astype(F32)


def row_of(halves_ref, row):
    left = halves_ref[pl.ds(row, FL, stride=ROWS), :]
    right = halves_ref[pl.ds(ROWS * FL + row, FL, stride=ROWS), :]
    return jnp.concatenate([left, right], axis=1)


def pack_kernel(scaled_in, msg_ref, scaled_ref):
    split_halves(scaled_in, scaled_ref)
    for row in range(0, ROWS, 2):
        pair = jnp.concatenate([row_of(scaled_ref, row), row_of(scaled_ref, row + 1)], axis=0)
        pair = pair * (1.0 / (1.0 + LEVELS[0] ** 2) ** 0.5)
        msg_ref[row * FL : (row + 2) * FL, :] = pair.astype(BF16)


def aux_kernel(
    count_ref, x_in, noise_in, step_ref, row_ref, col_ref, val_ref, aux_ref, x_ref, noise_ref,
    x_halves, noise_halves,
):
    split_halves(x_in, x_halves)
    split_halves(noise_in, noise_halves)
    for row in range(ROWS):
        x_ref[row * FL : (row + 1) * FL, :] = row_of(x_halves, row)
        noise_ref[row * FL : (row + 1) * FL, :] = row_of(noise_halves, row)
    for at, row in enumerate((0, ROWS - 2)):
        pair = noise_ref[row * FL : (row + 2) * FL, :]
        aux_ref[2 * at * FL : 2 * (at + 1) * FL, :] = pair.astype(BF16)
    live = iota((1, COLS), 1) < count_ref[...]
    cell = jnp.where(live, row_ref[...] * FL + step_ref[...] * 2, NO_CELL).astype(F32)
    val = val_ref[...]
    high = val.astype(BF16).astype(F32)
    middle = (val - high).astype(BF16).astype(F32)
    low = val - high - middle
    which = iota((16, COLS), 0)
    table = jnp.zeros((16, COLS), F32)
    for at, line in enumerate((cell, col_ref[...].astype(F32), high, middle, low)):
        table = jnp.where(which == at, line, table)
    aux_ref[AUX_OBS:AUX_ROWS, :] = table.astype(BF16)


def weights_kernel(n_tm, taps_ref, conv_out_ref, embed_ref, w1_ref, w2_ref, wide_ref):
    here = lax.axis_index("tm")
    even = lax.rem(here, 2) == 0
    has_far = jnp.logical_and(here > 0, here < n_tm - 1)
    wide_ref[...] = jnp.zeros(wide_ref.shape, F32)
    for at in range(9):
        tap = taps_ref[at].astype(F32)
        for frame in range(FRAMES):
            start = at * TAP_ROWS + 2 * frame
            wide_ref[start : start + TAPS, frame * 128 : frame * 128 + HID] = tap
    square = iota((HID, 128), 0) == iota((HID, 128), 1)
    line = jnp.concatenate([embed_ref[...], jnp.zeros((1, 128 - HID), F32)], axis=1)
    embed = jnp.sum(jnp.where(square, line, 0.0), axis=1, keepdims=True)
    high = embed.astype(BF16).astype(F32)
    middle = (embed - high).astype(BF16).astype(F32)
    low = embed - high - middle
    lane = iota((HID, DEPTH), 1) - (3 * NEAR + 3 * FL)
    bias = jnp.where(lane == 0, high, 0.0)
    bias = jnp.where(lane == 1, middle, bias)
    bias = jnp.where(lane == 2, low, bias)
    shape = (TAP_ROWS, DEPTH)
    lanes = iota(shape, 1)
    group = iota(shape, 0) >> 3
    within = iota(shape, 0) & 7
    slot = jnp.where(even, 2 - group, group)
    near = slot * FL + within
    far = jnp.where(has_far, 3 * NEAR + within, -DEPTH)
    parts = []
    for at in range(9):
        row_off, col_off = at // 3, at % 3
        near_start = row_off * NEAR + col_off * 2 * FL
        far_start = row_off * FAR + col_off * FL
        target = jnp.where(slot == 2, far + far_start, near + near_start)
        parts.append(jnp.where(lanes == target, 0.5, 0.0))
    move = jnp.concatenate(parts, axis=0).astype(BF16)
    for frame in range(FRAMES):
        taps = wide_ref[:, frame * 128 : (frame + 1) * 128].T[0:HID, :].astype(BF16)
        out = jnp.dot(taps, move, preferred_element_type=F32)
        w1_ref[frame * HID : (frame + 1) * HID, :] = (out + 0.5 * bias).astype(BF16)
    odd = iota((FL, HID), 0) % 2 == 1
    parts = []
    for at in range(9):
        upper = conv_out_ref[at, 0:1, :].astype(F32)
        lower = conv_out_ref[at, 1:2, :].astype(F32)
        parts.append(jnp.where(odd, lower, upper))
    stacked = jnp.concatenate(parts, axis=0).astype(BF16)
    shape = (HID, FRAMES * HID)
    spread = jnp.where(iota(shape, 1) % HID == iota(shape, 0), 1.0, 0.0).astype(BF16)
    tiled = jnp.dot(stacked, spread, preferred_element_type=F32)
    mine = (iota(tiled.shape, 0) % FL) // 2 == iota(tiled.shape, 1) // HID
    w2_ref[...] = jnp.where(mine, tiled, 0.0).astype(BF16)


def one_hot_maps(table, first_cell, cells):
    shape = (cells, COLS)
    hit = (iota(shape, 0) + first_cell).astype(F32) == table[0:1, :]
    lines = [jnp.where(hit, 1.0, 0.0)]
    for at in (2, 3, 4):
        lines.append(jnp.where(hit, table[at : at + 1, :], 0.0))
    lhs = jnp.concatenate(lines, axis=0).astype(BF16)
    cols_hot = jnp.where(iota((COLS, COLS), 0).astype(F32) == table[1:2, :], 1.0, 0.0)
    out = lax.dot_general(
        lhs, cols_hot.astype(BF16), (((1,), (1,)), ((), ())), preferred_element_type=F32
    )
    count = out[0:cells]
    total = out[cells : 2 * cells] + out[2 * cells : 3 * cells] + out[3 * cells : 4 * cells]
    return count, total


def maps_kernel(msg_ref, up_ref, down_ref, count_ref, total_ref):
    obs = slice(AUX_OBS, AUX_ROWS)
    pieces = (
        (up_ref, (ROWS - 2) * FL, 2 * FL, 0),
        (msg_ref, 0, ROWS * FL, 2 * FL),
        (down_ref, 0, 2 * FL, (ROWS + 2) * FL),
    )
    for ref, first_cell, cells, at in pieces:
        count, total = one_hot_maps(ref[obs, :].astype(F32), first_cell, cells)
        count_ref[at : at + cells, :] = count
        total_ref[at : at + cells, :] = total


def shifts(here):
    return [pltpu.roll(here, 1, 1), here, pltpu.roll(here, COLS - 1, 1)]


def near_kernel(core_ref, own_ref, near_ref):
    for pair in range(own_ref.shape[0] // (2 * FL)):
        at = slice(2 * pair * FL, 2 * (pair + 1) * FL)
        core, own = core_ref[at, :].astype(F32), own_ref[at, :].astype(F32)
        for sub in range(2):
            part = slice(sub * FL, (sub + 1) * FL)
            here = jnp.concatenate([core[part], own[part]], axis=0)
            block = jnp.concatenate(shifts(here), axis=0)
            start = (2 * pair + sub) * NEAR
            near_ref[start : start + NEAR, :] = block.astype(BF16)


def fill_pair(ref, win_ref, pair, level):
    far = ref[2 * pair * FL : 2 * (pair + 1) * FL, :].astype(F32)
    const = jnp.full((FL, COLS), level, F32)
    for sub in range(2):
        here = far[sub * FL : (sub + 1) * FL]
        block = jnp.concatenate(shifts(here) + [const], axis=0)
        start = (2 * pair + sub) * FAR
        win_ref[start : start + FAR, :] = block.astype(BF16)


def run_rows(near_ref, far_ref, w1_ref, w2_ref, win_ref, hid_ref, prod_ref, rows, level, emit):
    hidden_rows = rows - 2
    n = FRAMES * HID
    filled = 0
    for step in range(hidden_rows + LAG2 + LAG3):
        want = min(rows, step + 3 + AHEAD)
        while 2 * filled < want:
            fill_pair(far_ref, win_ref, filled, level)
            filled += 1
        if step < hidden_rows:
            near = near_ref[step * NEAR : (step + 3) * NEAR, :]
            far = win_ref[step * FAR : (step + 3) * FAR, :]
            window = jnp.concatenate([near, far], axis=0)
            half = jnp.dot(w1_ref[...], window, preferred_element_type=F32)
            hid_ref[step * n : (step + 1) * n, :] = (half + half * jnp.tanh(half)).astype(BF16)
        row = step - LAG2
        if 0 <= row < hidden_rows:
            prod_ref[row * 72 : (row + 1) * 72, :] = jnp.dot(
                w2_ref[...], hid_ref[row * n : (row + 1) * n, :], preferred_element_type=F32
            )
        row = step - LAG2 - LAG3
        if row >= 2:
            emit(row - 2)


def net_row(prod_ref, row):
    sums = []
    for col_off in range(3):
        acc = None
        for row_off in range(3):
            at = (row + row_off) * 72 + (3 * row_off + col_off) * FL
            term = prod_ref[at : at + FL, :]
            acc = term if acc is None else acc + term
        sums.append(acc)
    return pltpu.roll(sums[0], 1, 1) + sums[1] + pltpu.roll(sums[2], COLS - 1, 1)


def advance(x, noise, net, count, total, index):
    level, after = LEVELS[index], LEVELS[index + 1]
    spread = level**2 - after**2
    denoised = x * (1.0 / (1.0 + level**2)) + (level / (1.0 + level**2) ** 0.5) * net
    guide = (total - count * denoised) * (1.0 / (OBS_NOISE + COVARIANCE_GAIN * level**2))
    score = (denoised - x) * (1.0 / level**2) + guide
    return x + spread * score + spread**0.5 * noise


def first_kernel(
    x_ref, noise_ref, aux_up_ref, aux_down_ref, near_ref, own_ref, far_ref, w1_ref, w2_ref,
    count_ref, total_ref, next_ref, send_ref, win_ref, hid_ref, prod_ref,
):
    grow = (1.0 + LEVELS[0] ** 2) ** 0.5
    shrink = 1.0 / (1.0 + LEVELS[1] ** 2) ** 0.5
    made = {}

    def emit(here):
        part = slice((here % 2) * FL, (here % 2 + 1) * FL)
        if not 2 <= here < ROWS + 2:
            at = (here + 2) // 2 * 2 * FL
            x = own_ref[at : at + 2 * FL, :].astype(F32)[part] * grow
            ref, start = (aux_up_ref, 2 * FL) if here < 2 else (aux_down_ref, 0)
            noise = ref[start : start + 2 * FL, :].astype(F32)[part]
        else:
            inner = slice((here - 2) * FL, (here - 1) * FL)
            x, noise = x_ref[inner, :], noise_ref[inner, :]
        at = slice(here * FL, (here + 1) * FL)
        new = advance(x, noise, net_row(prod_ref, here), count_ref[at, :], total_ref[at, :], 0)
        if 2 <= here < ROWS + 2:
            next_ref[(here - 2) * FL : (here - 1) * FL, :] = new
        made[here % 2] = new
        if here % 2:
            pair = jnp.concatenate([made[0], made[1]], axis=0) * shrink
            send_ref[(here - 1) * FL : (here + 1) * FL, :] = pair.astype(BF16)

    run_rows(
        near_ref, far_ref, w1_ref, w2_ref, win_ref, hid_ref, prod_ref, 2 * ROWS, LEVELS[0], emit
    )


def second_kernel(
    x_ref, noise_in, near_ref, far_ref, w1_ref, w2_ref,
    count_ref, total_ref, out_ref, win_ref, hid_ref, prod_ref, noise_ref, half_ref,
):
    split_halves(noise_in, noise_ref)

    def emit(row):
        at = slice((row + 2) * FL, (row + 3) * FL)
        new = advance(
            x_ref[row * FL : (row + 1) * FL, :], row_of(noise_ref, row), net_row(prod_ref, row),
            count_ref[at, :], total_ref[at, :], 1,
        )
        half_ref[pl.ds(row, FL, stride=ROWS), :] = new[:, 0:128]
        half_ref[pl.ds(ROWS * FL + row, FL, stride=ROWS), :] = new[:, 128:256]

    run_rows(
        near_ref, far_ref, w1_ref, w2_ref, win_ref, hid_ref, prod_ref, ROWS + 4, LEVELS[1], emit
    )
    out_ref[:, 0:128] = half_ref[0 : ROWS * FL, :]
    out_ref[:, 128:256] = half_ref[ROWS * FL :, :]


def call(kernel, args, specs, outs, scratch=(), flops=0):
    moved = sum(a.size * a.dtype.itemsize for a in args)
    moved += sum(o.size * o.dtype.itemsize for o in outs)
    return pl.pallas_call(
        kernel,
        out_shape=tuple(outs),
        in_specs=specs,
        out_specs=tuple([VMEM] * len(outs)),
        scratch_shapes=list(scratch),
        compiler_params=params(),
        cost_estimate=pl.CostEstimate(flops=flops, bytes_accessed=moved, transcendentals=0),
    )(*args)


def time_pairs(n_tm, n_rows):
    core, far = [], []
    at = lambda i, r: i * n_rows + r
    for r in range(n_rows):
        for i in range(0, n_tm, 2):
            core += [(at(i, r), at(i + 1, r)), (at(i + 1, r), at(i, r))]
        for i in range(1, n_tm - 1, 2):
            far += [(at(i, r), at(i + 1, r)), (at(i + 1, r), at(i, r))]
        for i in (0, n_tm - 1):
            far.append((at(i, r), at(i, r ^ 1)))
    return core, far


def exchange_rows(block, n_rows):
    up = lax.ppermute(block, "rows", [(i, (i + 1) % n_rows) for i in range(n_rows)])
    if n_rows == 2:
        return up, up
    return up, lax.ppermute(block, "rows", [((i + 1) % n_rows, i) for i in range(n_rows)])


def exchange_time(block, n_tm, n_rows):
    core_pairs, far_pairs = time_pairs(n_tm, n_rows)
    far = lax.ppermute(block, ("tm", "rows"), far_pairs)
    core = lax.ppermute(block, ("tm", "rows"), core_pairs)
    return core, far


def scratch_for(rows):
    halves = pltpu.VMEM((2 * ROWS * FL, 128), F32)
    return [
        pltpu.VMEM((rows * FAR, COLS), BF16),
        pltpu.VMEM(((rows - 2) * FRAMES * HID, COLS), BF16),
        pltpu.VMEM(((rows - 2) * 72, COLS), F32),
        halves,
        halves,
    ]


def near_call(core, own):
    rows = own.shape[0] // FL
    (near,) = call(
        near_kernel, (core, own), [VMEM] * 2, [jax.ShapeDtypeStruct((rows * NEAR, COLS), BF16)]
    )
    return near


def first_call(*args):
    shape = jax.ShapeDtypeStruct
    return call(
        first_kernel,
        args,
        [VMEM] * 11,
        [shape((ROWS * FL, COLS), F32), shape(((ROWS + 4) * FL, COLS), BF16)],
        scratch_for(2 * ROWS)[:3],
        flops=14 * 2 * 256 * 384 * (256 + 72),
    )


def second_call(*args):
    (out,) = call(
        second_kernel,
        args,
        [VMEM] * 8,
        [jax.ShapeDtypeStruct((FL * ROWS, COLS), F32)],
        scratch_for(ROWS + 4),
        flops=10 * 2 * 256 * 384 * (256 + 72),
    )
    return out


def per_device(
    noisy_states, noise_first, noise_second, conv_in, conv_out, level_embed,
    obs_count, obs_step, obs_row, obs_col, obs_value,
):
    n_tm, n_rows = lax.axis_size("tm"), lax.axis_size("rows")
    frames, layers, rows, cols = noisy_states.shape
    assert frames == FRAMES and frames * layers == FL and rows == ROWS and cols == COLS
    assert n_tm % 2 == 0 and n_rows % 2 == 0 and obs_step.shape[-1] == COLS
    flat = lambda a: a.reshape(FL * ROWS, COLS)
    line = lambda a: a.reshape(1, -1)
    x, noise_a, noise_b = flat(noisy_states), flat(noise_first), flat(noise_second)
    shape = jax.ShapeDtypeStruct
    halves = pltpu.VMEM((2 * ROWS * FL, 128), F32)
    (msg,) = call(pack_kernel, (x,), [VMEM], [shape((ROWS * FL, COLS), BF16)], [halves])
    grid = shape((ROWS * FL, COLS), F32)
    aux, x_rows, noise_rows = call(
        aux_kernel,
        (obs_count, x, noise_a, line(obs_step), line(obs_row), line(obs_col), line(obs_value)),
        [VMEM] * 7,
        [shape((AUX_ROWS, COLS), BF16), grid, grid],
        [halves, halves],
    )
    up, down = exchange_rows(msg, n_rows)
    aux_up, aux_down = exchange_rows(aux, n_rows)
    w1, w2 = call(
        functools.partial(weights_kernel, n_tm),
        (conv_in.transpose(0, 2, 1), conv_out, line(level_embed)),
        [VMEM] * 3,
        [shape((FRAMES * HID, DEPTH), BF16), shape((72, FRAMES * HID), BF16)],
        [pltpu.VMEM((9 * TAP_ROWS, FRAMES * 128), F32)],
    )
    half = ROWS * FL // 2
    own = jnp.concatenate([up[half:], msg, down[:half]], axis=0)
    core, far = exchange_time(own, n_tm, n_rows)
    maps = shape(((ROWS + 4) * FL, COLS), F32)
    count, total = call(maps_kernel, (aux, aux_up, aux_down), [VMEM] * 3, [maps, maps])
    near = near_call(core, own)
    current, send = first_call(
        x_rows, noise_rows, aux_up, aux_down, near, own, far, w1, w2, count, total
    )
    core, far = exchange_time(send, n_tm, n_rows)
    near = near_call(core, send)
    out = second_call(current, noise_b, near, far, w1, w2, count, total)
    return out.reshape(noisy_states.shape)


def solution(mesh):
    states = P("tm", None, "rows", None)
    slots = P("tm", "rows", None)
    in_specs = (states, states, states, P(), P(), P(), P("tm", "rows"), slots, slots, slots, slots)
    return jax.shard_map(
        per_device, mesh=mesh, in_specs=in_specs, out_specs=states, check_vma=False
    )
```

```python
import functools

import jax
import jax.numpy as jnp
from jax import lax
from jax.experimental import pallas as pl
from jax.experimental.pallas import tpu as pltpu
from jax.sharding import PartitionSpec as P


LEVELS = (1.0, 0.5, 0.2)
OBS_NOISE = 0.1
COVARIANCE_GAIN = 0.5

FL = 8
ROWS = 8
COLS = 256
HID = 96
FRAMES = 4
NEAR = 48
FAR = 32
TAPS = 18
TAP_ROWS = 24
DEPTH = 3 * (NEAR + FAR)
AUX_OBS = 4 * FL
AUX_ROWS = AUX_OBS + 16
NO_CELL = 64
AHEAD, LAG2, LAG3 = 4, 4, 4
VMEM = pl.BlockSpec(memory_space=pltpu.VMEM)
F32 = jnp.float32
BF16 = jnp.bfloat16


def params():
    return pltpu.CompilerParams(vmem_limit_bytes=16 * 1024 * 1024)


def iota(shape, dim):
    return lax.broadcasted_iota(jnp.int32, shape, dim)


def split_halves(ref, halves_ref):
    halves_ref[0 : ROWS * FL, :] = ref[:, 0:128].astype(F32)
    halves_ref[ROWS * FL :, :] = ref[:, 128:256].astype(F32)


def row_of(halves_ref, row):
    left = halves_ref[pl.ds(row, FL, stride=ROWS), :]
    right = halves_ref[pl.ds(ROWS * FL + row, FL, stride=ROWS), :]
    return jnp.concatenate([left, right], axis=1)


def pack_kernel(scaled_in, msg_ref, scaled_ref):
    split_halves(scaled_in, scaled_ref)
    for row in range(0, ROWS, 2):
        pair = jnp.concatenate([row_of(scaled_ref, row), row_of(scaled_ref, row + 1)], axis=0)
        msg_ref[row * FL : (row + 2) * FL, :] = pair.astype(BF16)


def aux_kernel(
    count_ref, x_in, noise_in, step_ref, row_ref, col_ref, val_ref, aux_ref, x_ref, noise_ref,
    x_halves, noise_halves,
):
    split_halves(x_in, x_halves)
    split_halves(noise_in, noise_halves)
    for row in range(ROWS):
        x_ref[row * FL : (row + 1) * FL, :] = row_of(x_halves, row)
        noise_ref[row * FL : (row + 1) * FL, :] = row_of(noise_halves, row)
    for at, row in enumerate((0, ROWS - 2)):
        pair = noise_ref[row * FL : (row + 2) * FL, :]
        aux_ref[2 * at * FL : 2 * (at + 1) * FL, :] = pair.astype(BF16)
    live = iota((1, COLS), 1) < count_ref[...]
    cell = jnp.where(live, row_ref[...] * FL + step_ref[...] * 2, NO_CELL).astype(F32)
    val = val_ref[...]
    high = val.astype(BF16).astype(F32)
    middle = (val - high).astype(BF16).astype(F32)
    low = val - high - middle
    which = iota((16, COLS), 0)
    table = jnp.zeros((16, COLS), F32)
    for at, line in enumerate((cell, col_ref[...].astype(F32), high, middle, low)):
        table = jnp.where(which == at, line, table)
    aux_ref[AUX_OBS:AUX_ROWS, :] = table.astype(BF16)


def weights_kernel(n_tm, taps_ref, conv_out_ref, embed_ref, w1_ref, w2_ref, wide_ref):
    here = lax.axis_index("tm")
    even = lax.rem(here, 2) == 0
    has_far = jnp.logical_and(here > 0, here < n_tm - 1)
    wide_ref[...] = jnp.zeros(wide_ref.shape, F32)
    for at in range(9):
        tap = taps_ref[at].astype(F32)
        for frame in range(FRAMES):
            start = at * TAP_ROWS + 2 * frame
            wide_ref[start : start + TAPS, frame * 128 : frame * 128 + HID] = tap
    square = iota((HID, 128), 0) == iota((HID, 128), 1)
    line = jnp.concatenate([embed_ref[...], jnp.zeros((1, 128 - HID), F32)], axis=1)
    embed = jnp.sum(jnp.where(square, line, 0.0), axis=1, keepdims=True)
    high = embed.astype(BF16).astype(F32)
    middle = (embed - high).astype(BF16).astype(F32)
    low = embed - high - middle
    lane = iota((HID, DEPTH), 1) - (3 * NEAR + 3 * FL)
    bias = jnp.where(lane == 0, high, 0.0)
    bias = jnp.where(lane == 1, middle, bias)
    bias = jnp.where(lane == 2, low, bias)
    shape = (TAP_ROWS, DEPTH)
    lanes = iota(shape, 1)
    group = iota(shape, 0) >> 3
    within = iota(shape, 0) & 7
    slot = jnp.where(even, 2 - group, group)
    near = slot * FL + within
    far = jnp.where(has_far, 3 * NEAR + within, -DEPTH)
    parts = []
    for at in range(9):
        row_off, col_off = at // 3, at % 3
        near_start = row_off * NEAR + col_off * 2 * FL
        far_start = row_off * FAR + col_off * FL
        target = jnp.where(slot == 2, far + far_start, near + near_start)
        parts.append(jnp.where(lanes == target, 0.5, 0.0))
    move = jnp.concatenate(parts, axis=0).astype(BF16)
    for frame in range(FRAMES):
        taps = wide_ref[:, frame * 128 : (frame + 1) * 128].T[0:HID, :].astype(BF16)
        out = jnp.dot(taps, move, preferred_element_type=F32)
        w1_ref[frame * HID : (frame + 1) * HID, :] = (out + 0.5 * bias).astype(BF16)
    odd = iota((FL, HID), 0) % 2 == 1
    parts = []
    for at in range(9):
        upper = conv_out_ref[at, 0:1, :].astype(F32)
        lower = conv_out_ref[at, 1:2, :].astype(F32)
        parts.append(jnp.where(odd, lower, upper))
    stacked = jnp.concatenate(parts, axis=0).astype(BF16)
    shape = (HID, FRAMES * HID)
    spread = jnp.where(iota(shape, 1) % HID == iota(shape, 0), 1.0, 0.0).astype(BF16)
    tiled = jnp.dot(stacked, spread, preferred_element_type=F32)
    mine = (iota(tiled.shape, 0) % FL) // 2 == iota(tiled.shape, 1) // HID
    w2_ref[...] = jnp.where(mine, tiled, 0.0).astype(BF16)


def one_hot_maps(table, first_cell, cells):
    shape = (cells, COLS)
    hit = (iota(shape, 0) + first_cell).astype(F32) == table[0:1, :]
    lines = [jnp.where(hit, 1.0, 0.0)]
    for at in (2, 3, 4):
        lines.append(jnp.where(hit, table[at : at + 1, :], 0.0))
    lhs = jnp.concatenate(lines, axis=0).astype(BF16)
    cols_hot = jnp.where(iota((COLS, COLS), 0).astype(F32) == table[1:2, :], 1.0, 0.0)
    out = lax.dot_general(
        lhs, cols_hot.astype(BF16), (((1,), (1,)), ((), ())), preferred_element_type=F32
    )
    count = out[0:cells]
    total = out[cells : 2 * cells] + out[2 * cells : 3 * cells] + out[3 * cells : 4 * cells]
    return count, total


def maps_kernel(msg_ref, up_ref, down_ref, count_ref, total_ref):
    obs = slice(AUX_OBS, AUX_ROWS)
    pieces = (
        (up_ref, (ROWS - 2) * FL, 2 * FL, 0),
        (msg_ref, 0, ROWS * FL, 2 * FL),
        (down_ref, 0, 2 * FL, (ROWS + 2) * FL),
    )
    for ref, first_cell, cells, at in pieces:
        count, total = one_hot_maps(ref[obs, :].astype(F32), first_cell, cells)
        count_ref[at : at + cells, :] = count
        total_ref[at : at + cells, :] = total


def shifts(here):
    return [pltpu.roll(here, 1, 1), here, pltpu.roll(here, COLS - 1, 1)]


def near_kernel(core_ref, own_ref, near_ref):
    for pair in range(own_ref.shape[0] // (2 * FL)):
        at = slice(2 * pair * FL, 2 * (pair + 1) * FL)
        core, own = core_ref[at, :].astype(F32), own_ref[at, :].astype(F32)
        for sub in range(2):
            part = slice(sub * FL, (sub + 1) * FL)
            here = jnp.concatenate([core[part], own[part]], axis=0)
            block = jnp.concatenate(shifts(here), axis=0)
            start = (2 * pair + sub) * NEAR
            near_ref[start : start + NEAR, :] = block.astype(BF16)


def fill_pair(ref, win_ref, pair, level):
    far = ref[2 * pair * FL : 2 * (pair + 1) * FL, :].astype(F32)
    const = jnp.full((FL, COLS), level, F32)
    for sub in range(2):
        here = far[sub * FL : (sub + 1) * FL]
        block = jnp.concatenate(shifts(here) + [const], axis=0)
        start = (2 * pair + sub) * FAR
        win_ref[start : start + FAR, :] = block.astype(BF16)


def run_rows(near_ref, far_ref, w1_ref, w2_ref, win_ref, hid_ref, prod_ref, rows, level, emit):
    hidden_rows = rows - 2
    n = FRAMES * HID
    filled = 0
    for step in range(hidden_rows + LAG2 + LAG3):
        want = min(rows, step + 3 + AHEAD)
        while 2 * filled < want:
            fill_pair(far_ref, win_ref, filled, level)
            filled += 1
        if step < hidden_rows:
            near = near_ref[step * NEAR : (step + 3) * NEAR, :]
            far = win_ref[step * FAR : (step + 3) * FAR, :]
            window = jnp.concatenate([near, far], axis=0)
            half = jnp.dot(w1_ref[...], window, preferred_element_type=F32)
            hid_ref[step * n : (step + 1) * n, :] = (half + half * jnp.tanh(half)).astype(BF16)
        row = step - LAG2
        if 0 <= row < hidden_rows:
            first_off = max(0, row - (hidden_rows - 3))
            last_off = min(2, row)
            used = slice(first_off * 24, (last_off + 1) * 24)
            prod_ref[row * 72 + used.start : row * 72 + used.stop, :] = jnp.dot(
                w2_ref[used, :], hid_ref[row * n : (row + 1) * n, :], preferred_element_type=F32
            )
        row = step - LAG2 - LAG3
        if row >= 2:
            emit(row - 2)


def net_row(prod_ref, row):
    sums = []
    for col_off in range(3):
        acc = None
        for row_off in range(3):
            at = (row + row_off) * 72 + (3 * row_off + col_off) * FL
            term = prod_ref[at : at + FL, :]
            acc = term if acc is None else acc + term
        sums.append(acc)
    return pltpu.roll(sums[0], 1, 1) + sums[1] + pltpu.roll(sums[2], COLS - 1, 1)


def advance(x, noise, net, count, total, index):
    level, after = LEVELS[index], LEVELS[index + 1]
    spread = level**2 - after**2
    denoised = x * (1.0 / (1.0 + level**2)) + (level / (1.0 + level**2) ** 0.5) * net
    guide = (total - count * denoised) * (1.0 / (OBS_NOISE + COVARIANCE_GAIN * level**2))
    score = (denoised - x) * (1.0 / level**2) + guide
    return x + spread * score + spread**0.5 * noise


def first_kernel(
    x_ref, noise_ref, aux_up_ref, aux_down_ref, near_ref, own_ref, far_ref, w1_ref, w2_ref,
    count_ref, total_ref, next_ref, send_ref, win_ref, hid_ref, prod_ref,
):
    grow = (1.0 + LEVELS[0] ** 2) ** 0.5
    shrink = 1.0 / (1.0 + LEVELS[1] ** 2) ** 0.5
    made = {}

    def emit(here):
        part = slice((here % 2) * FL, (here % 2 + 1) * FL)
        if not 2 <= here < ROWS + 2:
            at = (here + 2) // 2 * 2 * FL
            x = own_ref[at : at + 2 * FL, :].astype(F32)[part] * grow
            ref, start = (aux_up_ref, 2 * FL) if here < 2 else (aux_down_ref, 0)
            noise = ref[start : start + 2 * FL, :].astype(F32)[part]
        else:
            inner = slice((here - 2) * FL, (here - 1) * FL)
            x, noise = x_ref[inner, :], noise_ref[inner, :]
        at = slice(here * FL, (here + 1) * FL)
        new = advance(x, noise, net_row(prod_ref, here), count_ref[at, :], total_ref[at, :], 0)
        if 2 <= here < ROWS + 2:
            next_ref[(here - 2) * FL : (here - 1) * FL, :] = new
        made[here % 2] = new
        if here % 2:
            pair = jnp.concatenate([made[0], made[1]], axis=0) * shrink
            send_ref[(here - 1) * FL : (here + 1) * FL, :] = pair.astype(BF16)

    run_rows(
        near_ref, far_ref, w1_ref, w2_ref, win_ref, hid_ref, prod_ref, 2 * ROWS, LEVELS[0], emit
    )


def second_kernel(
    x_ref, noise_in, near_ref, far_ref, w1_ref, w2_ref,
    count_ref, total_ref, out_ref, win_ref, hid_ref, prod_ref, noise_ref, half_ref,
):
    split_halves(noise_in, noise_ref)

    def emit(row):
        at = slice((row + 2) * FL, (row + 3) * FL)
        new = advance(
            x_ref[row * FL : (row + 1) * FL, :], row_of(noise_ref, row), net_row(prod_ref, row),
            count_ref[at, :], total_ref[at, :], 1,
        )
        half_ref[pl.ds(row, FL, stride=ROWS), :] = new[:, 0:128]
        half_ref[pl.ds(ROWS * FL + row, FL, stride=ROWS), :] = new[:, 128:256]

    run_rows(
        near_ref, far_ref, w1_ref, w2_ref, win_ref, hid_ref, prod_ref, ROWS + 4, LEVELS[1], emit
    )
    out_ref[:, 0:128] = half_ref[0 : ROWS * FL, :]
    out_ref[:, 128:256] = half_ref[ROWS * FL :, :]


def call(kernel, args, specs, outs, scratch=(), flops=0):
    moved = sum(a.size * a.dtype.itemsize for a in args)
    moved += sum(o.size * o.dtype.itemsize for o in outs)
    return pl.pallas_call(
        kernel,
        out_shape=tuple(outs),
        in_specs=specs,
        out_specs=tuple([VMEM] * len(outs)),
        scratch_shapes=list(scratch),
        compiler_params=params(),
        cost_estimate=pl.CostEstimate(flops=flops, bytes_accessed=moved, transcendentals=0),
    )(*args)


def time_pairs(n_tm, n_rows):
    core, far = [], []
    at = lambda i, r: i * n_rows + r
    for r in range(n_rows):
        for i in range(0, n_tm, 2):
            core += [(at(i, r), at(i + 1, r)), (at(i + 1, r), at(i, r))]
        for i in range(1, n_tm - 1, 2):
            far += [(at(i, r), at(i + 1, r)), (at(i + 1, r), at(i, r))]
        for i in (0, n_tm - 1):
            far.append((at(i, r), at(i, r ^ 1)))
    return core, far


def exchange_rows(block, n_rows):
    up = lax.ppermute(block, "rows", [(i, (i + 1) % n_rows) for i in range(n_rows)])
    if n_rows == 2:
        return up, up
    return up, lax.ppermute(block, "rows", [((i + 1) % n_rows, i) for i in range(n_rows)])


def exchange_time(block, n_tm, n_rows):
    core_pairs, far_pairs = time_pairs(n_tm, n_rows)
    far = lax.ppermute(block, ("tm", "rows"), far_pairs)
    core = lax.ppermute(block, ("tm", "rows"), core_pairs)
    return core, far


def scratch_for(rows):
    halves = pltpu.VMEM((2 * ROWS * FL, 128), F32)
    return [
        pltpu.VMEM((rows * FAR, COLS), BF16),
        pltpu.VMEM(((rows - 2) * FRAMES * HID, COLS), BF16),
        pltpu.VMEM(((rows - 2) * 72, COLS), F32),
        halves,
        halves,
    ]


def near_call(core, own):
    rows = own.shape[0] // FL
    (near,) = call(
        near_kernel, (core, own), [VMEM] * 2, [jax.ShapeDtypeStruct((rows * NEAR, COLS), BF16)]
    )
    return near


def first_call(*args):
    shape = jax.ShapeDtypeStruct
    return call(
        first_kernel,
        args,
        [VMEM] * 11,
        [shape((ROWS * FL, COLS), F32), shape(((ROWS + 4) * FL, COLS), BF16)],
        scratch_for(2 * ROWS)[:3],
        flops=14 * 2 * 256 * 384 * (256 + 72),
    )


def second_call(*args):
    (out,) = call(
        second_kernel,
        args,
        [VMEM] * 8,
        [jax.ShapeDtypeStruct((FL * ROWS, COLS), F32)],
        scratch_for(ROWS + 4),
        flops=10 * 2 * 256 * 384 * (256 + 72),
    )
    return out


def per_device(
    noisy_states, noise_first, noise_second, conv_in, conv_out, level_embed,
    obs_count, obs_step, obs_row, obs_col, obs_value,
):
    n_tm, n_rows = lax.axis_size("tm"), lax.axis_size("rows")
    frames, layers, rows, cols = noisy_states.shape
    assert frames == FRAMES and frames * layers == FL and rows == ROWS and cols == COLS
    assert n_tm % 2 == 0 and n_rows % 2 == 0 and obs_step.shape[-1] == COLS
    flat = lambda a: a.reshape(FL * ROWS, COLS)
    line = lambda a: a.reshape(1, -1)
    x, noise_a, noise_b = flat(noisy_states), flat(noise_first), flat(noise_second)
    shape = jax.ShapeDtypeStruct
    scaled = (x / (1.0 + LEVELS[0] ** 2) ** 0.5).astype(BF16)
    halves = pltpu.VMEM((2 * ROWS * FL, 128), F32)
    (msg,) = call(pack_kernel, (scaled,), [VMEM], [shape((ROWS * FL, COLS), BF16)], [halves])
    grid = shape((ROWS * FL, COLS), F32)
    aux, x_rows, noise_rows = call(
        aux_kernel,
        (obs_count, x, noise_a, line(obs_step), line(obs_row), line(obs_col), line(obs_value)),
        [VMEM] * 7,
        [shape((AUX_ROWS, COLS), BF16), grid, grid],
        [halves, halves],
    )
    up, down = exchange_rows(msg, n_rows)
    aux_up, aux_down = exchange_rows(aux, n_rows)
    w1, w2 = call(
        functools.partial(weights_kernel, n_tm),
        (conv_in.transpose(0, 2, 1), conv_out, line(level_embed)),
        [VMEM] * 3,
        [shape((FRAMES * HID, DEPTH), BF16), shape((72, FRAMES * HID), BF16)],
        [pltpu.VMEM((9 * TAP_ROWS, FRAMES * 128), F32)],
    )
    half = ROWS * FL // 2
    own = jnp.concatenate([up[half:], msg, down[:half]], axis=0)
    core, far = exchange_time(own, n_tm, n_rows)
    maps = shape(((ROWS + 4) * FL, COLS), F32)
    count, total = call(maps_kernel, (aux, aux_up, aux_down), [VMEM] * 3, [maps, maps])
    near = near_call(core, own)
    current, send = first_call(
        x_rows, noise_rows, aux_up, aux_down, near, own, far, w1, w2, count, total
    )
    core, far = exchange_time(send, n_tm, n_rows)
    near = near_call(core, send)
    out = second_call(current, noise_b, near, far, w1, w2, count, total)
    return out.reshape(noisy_states.shape)


def solution(mesh):
    states = P("tm", None, "rows", None)
    slots = P("tm", "rows", None)
    in_specs = (states, states, states, P(), P(), P(), P("tm", "rows"), slots, slots, slots, slots)
    return jax.shard_map(
        per_device, mesh=mesh, in_specs=in_specs, out_specs=states, check_vma=False
    )
```
